32 devices in a mesh: inst: 16 (over z, y, x), cells: 2 (over core).
Axes of the slice: x: 2, y: 2, z: 4, core: 2. Of those that a mesh axis runs over, the one named last changes fastest.
Arguments:
- adjoint: float32 [16, 5, 8, 16, 128], P('inst', None, 'cells'), may hold values from -6 to 6
- objective_gradient: float32 [16, 5, 8, 16, 128], P('inst', None, 'cells'), may hold values from -6 to 6
- jacobian: float32 [16, 3, 5, 5, 8, 16, 128], P('inst', None, None, None, 'cells'), may hold values from -2.5 to 2.5
- second_coef: float32 [16, 3, 8, 16, 128], P('inst', None, 'cells'), may hold values from 0.05 to 0.5
- fourth_coef: float32 [16, 3, 8, 16, 128], P('inst', None, 'cells'), may hold values from 0.01 to 0.1
- time_step: float32 [16, 8, 16, 128], P('inst', 'cells'), may hold values from 0.03 to 0.15
- frequency: float32 [1], replicated, may hold values from 0.5 to 1.5
- damping: float32 [1], replicated, may hold values from 0.02 to 0.08
Outputs:
- updated: float32 [16, 5, 8, 16, 128], P('inst', None, 'cells')
The draws below stay inside these ranges and needn't reach their ends.
All inputs are finite; a program needn't handle non-finite values.
Results may differ from the reference program's by a relative error of at most 0.0001.
Values sent between devices are 32-bit elements; how exact they have to be, the bound alone decides.
A program may use at most 64 MiB of HBM per device.

```python
import math
import jax
import jax.numpy as jnp
from jax import lax

INSTANCES = 16
VARS = 5
NY = 16
NZ = 128
NX = 8


def block_scale(own_key, shape, shards, low, largest):
    level = 1.0
    for dim, parts in shards:
        heights = jax.random.uniform(jax.random.fold_in(jax.random.fold_in(own_key, 6), dim), (parts,), jnp.float32, low / len(shards), largest / len(shards))
        level = level * jnp.repeat(jnp.exp(heights), shape[dim] // parts).reshape((-1,) + (1,) * (len(shape) - 1 - dim))
    return level


def gaussian(stream_key, dims, width, bound, split=(), kind=jnp.bfloat16):
    values = width * jax.random.normal(stream_key, dims, jnp.float32)
    if split:
        values = values * block_scale(stream_key, dims, split, -0.22, 0.18)
    return jnp.clip(values, -bound, bound).astype(kind)


def setup_inputs(seed: int = 0) -> dict:
    keys = jax.random.split(jax.random.key(seed), 9)
    return {
        "adjoint": gaussian(keys[0], (INSTANCES, VARS, NX, NY, NZ), 1.0, 6.0, ((0, 16), (2, 2)), jnp.float32),
        "objective_gradient": gaussian(keys[1], (INSTANCES, VARS, NX, NY, NZ), 1.0, 6.0, ((0, 16), (2, 2)), jnp.float32),
        "jacobian": gaussian(keys[2], (INSTANCES, 3, VARS, VARS, NX, NY, NZ), VARS ** -0.5, 2.5, ((0, 16), (4, 2)), jnp.float32),
        "second_coef": jnp.clip(jnp.exp(math.log(0.5) - 2.3025851 * jax.random.uniform(keys[3], (INSTANCES, 3, NX, NY, NZ), jnp.float32) ** block_scale(keys[3], (INSTANCES, 3, NX, NY, NZ), ((0, 16), (2, 2)), -0.2, 0.2)), 0.05, 0.5),
        "fourth_coef": jnp.clip(jnp.exp(math.log(0.1) - 2.3025851 * jax.random.uniform(keys[4], (INSTANCES, 3, NX, NY, NZ), jnp.float32) ** block_scale(keys[4], (INSTANCES, 3, NX, NY, NZ), ((0, 16), (2, 2)), -0.2, 0.2)), 0.01, 0.1),
        "time_step": jnp.clip(jnp.exp(math.log(0.15) - 1.609438 * jax.random.uniform(keys[5], (INSTANCES, NX, NY, NZ), jnp.float32) ** block_scale(keys[5], (INSTANCES, NX, NY, NZ), ((0, 16), (1, 2)), -0.2, 0.2)), 0.03, 0.15),
        "frequency": jnp.clip(jnp.exp(jax.random.uniform(keys[6], (1,), jnp.float32, math.log(0.5), math.log(1.5))), 0.5, 1.5),
        "damping": jnp.clip(jnp.exp(jax.random.uniform(keys[7], (1,), jnp.float32, math.log(0.02), math.log(0.08))), 0.02, 0.08),
    }


def spectral_coupling(frequency_value, damping_value, count):
    positions = jnp.arange(count, dtype=jnp.int32)
    offsets = positions[:, None] - positions[None, :]
    parity = jnp.where(offsets % 2 == 0, 1.0, -1.0).astype(jnp.float32)
    angle = (math.pi / count) * offsets.astype(jnp.float32)
    off_diag = offsets != 0
    sine = jnp.where(off_diag, jnp.sin(angle), 1.0)
    slope = jnp.where(off_diag, 0.5 * parity * jnp.cos(angle) / sine, 0.0)
    curve = jnp.where(off_diag, parity * 0.5 / (sine * sine), count * count / 12.0 + 1.0 / 6.0)
    return (frequency_value * slope + damping_value * curve).astype(jnp.float32)


def face_terms(padded, second_pad, fourth_pad, grid_axis):
    length = padded.shape[grid_axis] - 4

    def cut(source, first, size):
        return lax.slice_in_dim(source, first, first + size, axis=grid_axis)

    jumps = cut(padded, 1, length + 3) - cut(padded, 0, length + 3)
    second_flux = cut(second_pad, 0, length + 3) * jumps
    fourth_flux = cut(fourth_pad, 0, length + 3) * jumps
    divided = cut(fourth_flux, 1, length + 2) - cut(fourth_flux, 0, length + 2)
    central = 0.5 * (cut(padded, 1, length) - cut(padded, 3, length))
    damped = cut(second_flux, 1, length) - cut(second_flux, 2, length)
    damped = damped + cut(divided, 2, length) - 2.0 * cut(divided, 1, length) + cut(divided, 0, length)
    return central, damped


def spatial_one(inputs):
    section_state, jac_one, second_one, fourth_one = inputs
    summed = jnp.zeros_like(section_state)
    for direction in range(3):
        grid_axis = 1 + direction
        widths = [(0, 0), (0, 0), (0, 0), (0, 0)]
        widths[grid_axis] = (2, 2)
        padded = jnp.pad(section_state, widths)
        second_pad = jnp.pad(second_one[direction][None], widths)
        fourth_pad = jnp.pad(fourth_one[direction][None], widths)
        central, damped = face_terms(padded, second_pad, fourth_pad, grid_axis)
        summed = summed + jnp.sum(jac_one[direction] * central[:, None], axis=0) + damped
    return summed


def reference(adjoint, objective_gradient, jacobian, second_coef, fourth_coef, time_step, frequency, damping):
    coupling = spectral_coupling(frequency[0], damping[0], INSTANCES)
    section_state = adjoint
    for section_coef in (0.25, 1.0 / 6.0, 0.375, 0.5, 1.0):
        spatial = lax.map(spatial_one, (section_state, jacobian, second_coef, fourth_coef))
        coupled = jnp.einsum("jk,jvxyz->kvxyz", coupling, section_state, precision=lax.Precision.HIGHEST)
        residual = spatial + coupled + objective_gradient
        section_state = adjoint - section_coef * time_step[:, None] * residual
    return section_state
```

```python
import functools
import math

import jax
import jax.numpy as jnp
from jax import lax
from jax.experimental import pallas as pl
from jax.experimental.pallas import tpu as pltpu
from jax.sharding import PartitionSpec as P

FACTORS = (0.25, 1.0 / 6.0, 0.375, 0.5, 1.0)
SECTIONS = len(FACTORS)
PAD = 8
TILE = 8
MESH = pl.DeviceIdType.MESH


def coupling_tables(count):
    slope, curve = [0.0], [count * count / 12.0 + 1.0 / 6.0]
    for m in range(1, count):
        parity = 1.0 if m % 2 == 0 else -1.0
        angle = math.pi * m / count
        slope.append(0.5 * parity * math.cos(angle) / math.sin(angle))
        curve.append(0.5 * parity / math.sin(angle) ** 2)
    return slope, curve


def kernel(
    n, cells, adj, grad, jac, c2, c4, dt, freq_in, damp_in, out,
    vp, jv, cx, cy, cz, kk, gv, uh, mh, tb, mt, hb, kv, freq, damp,
    loc_sem, ss, trs, mrs, hss, hrs, chs, chr_,
):
    nv, lay, ny, nz = adj.shape
    rows = lay * ny // n
    per = ny // rows
    pack = TILE // rows
    groups = n // pack
    me = lax.axis_index("inst")
    cell = lax.axis_index("cells")
    has_lo = cell > 0
    has_hi = cell < cells - 1
    lo = has_lo.astype(jnp.int32)
    hi = has_hi.astype(jnp.int32)
    both = lo * hi
    back = lo * (1 - both)
    mid = slice(PAD, PAD + ny)

    def mirror(value, step, count):
        if count & (count - 1):
            return lax.rem(value + 1 + step, count)
        flip, total, bit = count - 1 - step, 0, 1
        while bit < count:
            total = total + lax.rem(value // bit + flip // bit, 2) * bit
            bit *= 2
        return total

    barrier = pltpu.get_barrier_semaphore()

    @pl.loop(0, n - 1)
    def _(i):
        pl.semaphore_signal(barrier, inc=1, device_id={"inst": mirror(me, i, n)}, device_id_type=MESH)

    @pl.when(has_lo)
    def _():
        pl.semaphore_signal(barrier, inc=1, device_id={"cells": cell - 1}, device_id_type=MESH)

    @pl.when(has_hi)
    def _():
        pl.semaphore_signal(barrier, inc=1, device_id={"cells": cell + 1}, device_id_type=MESH)

    local = [
        (adj, vp.at[0, :, 2 : 2 + lay, mid, :]),
        (dt, uh.at[0, nv]),
        (c2.at[0], cx.at[0, 2 : 2 + lay]),
        (c4.at[0], cx.at[1, 2 : 2 + lay]),
        (c2.at[1], cy.at[0, :, mid, :]),
        (c4.at[1], cy.at[1, :, mid, :]),
        (c2.at[2], cz.at[0]),
        (c4.at[2], cz.at[1]),
        (grad, gv),
        (jac, jv),
        (freq_in, freq),
        (damp_in, damp),
    ]
    local = [pltpu.make_async_copy(s, d, loc_sem.at[i]) for i, (s, d) in enumerate(local)]
    for c in local:
        c.start()
    dtv = uh.at[0, nv]

    def wait_bytes(ref, sem):
        pltpu.make_async_copy(ref, ref, sem).wait()

    def width(unit):
        return nv + 1 if unit == 1 else nv

    def spot(p):
        return lax.rem(p, lay), pl.multiple_of((p // lay) * rows, rows)

    def owner_rows(p):
        return pl.ds(pl.multiple_of(p * rows, rows), rows)

    def outbound(unit, p):
        x, y = spot(p)
        if unit == 0:
            src = vp.at[0, :, 2 + x, pl.ds(PAD + y, rows), :]
        else:
            src = uh.at[unit - 1, 0 : width(unit), x, pl.ds(y, rows), :]
        return src, tb.at[unit, 0 : width(unit), owner_rows(me), :]

    def send_out(unit, p):
        src, dst = outbound(unit, p)

        @pl.when(p != me)
        def _():
            pltpu.make_async_remote_copy(
                src_ref=src, dst_ref=dst, send_sem=ss.at[unit], recv_sem=trs.at[unit],
                device_id={"inst": p}, device_id_type=MESH,
            ).start()

        @pl.when(p == me)
        def _():
            pltpu.make_async_copy(src, dst, trs.at[unit]).start()

    def send_home(s):
        x, y = spot(me)
        dst = mh.at[s, :, x, pl.ds(y, rows), :]

        @pl.loop(0, n - 1)
        def _(i):
            p = mirror(me, i, n)
            pltpu.make_async_remote_copy(
                src_ref=mt.at[s, :, owner_rows(p), :], dst_ref=dst,
                send_sem=ss.at[SECTIONS + s], recv_sem=mrs.at[s, x],
                device_id={"inst": p}, device_id_type=MESH,
            ).start()

        pltpu.make_async_copy(mt.at[s, :, owner_rows(me), :], dst, mrs.at[s, x]).start()

    def halo_up(s):
        return pltpu.make_async_remote_copy(
            src_ref=vp.at[s, :, lay : lay + 2, mid, :], dst_ref=hb.at[s, 0],
            send_sem=hss.at[s, 0], recv_sem=hrs.at[s, 0],
            device_id={"cells": cell + 1}, device_id_type=MESH,
        )

    def halo_down(s):
        return pltpu.make_async_remote_copy(
            src_ref=vp.at[s, :, 2:4, mid, :], dst_ref=hb.at[s, 1],
            send_sem=hss.at[s, 1], recv_sem=hrs.at[s, 1],
            device_id={"cells": cell - 1}, device_id_type=MESH,
        )

    coef_up = pltpu.make_async_remote_copy(
        src_ref=cx.at[:, lay : lay + 2], dst_ref=cx.at[:, 0:2],
        send_sem=chs.at[0], recv_sem=chr_.at[0],
        device_id={"cells": cell + 1}, device_id_type=MESH,
    )
    coef_down = pltpu.make_async_remote_copy(
        src_ref=cx.at[:, 2:4], dst_ref=cx.at[:, 2 + lay : 4 + lay],
        send_sem=chs.at[1], recv_sem=chr_.at[1],
        device_id={"cells": cell - 1}, device_id_type=MESH,
    )

    def start_pair(up, down):
        @pl.when(has_hi)
        def _():
            up.start()

        @pl.when(has_lo)
        def _():
            down.start()

    def land_pair(up, down):
        @pl.when(has_lo)
        def _():
            up.wait_recv()

        @pl.when(has_hi)
        def _():
            down.wait_recv()

    def sent_pair(up, down):
        @pl.when(has_hi)
        def _():
            up.wait_send()

        @pl.when(has_lo)
        def _():
            down.wait_send()

    lanes = lax.broadcasted_iota(jnp.int32, (ny, nz), 1)
    keep_lo = jnp.where(lanes >= 1, 1.0, 0.0)
    keep_hi = jnp.where(lanes < nz - 1, 1.0, 0.0)

    def stencil_plane():
        @pl.loop(0, lay)
        def _(x):
            up4 = cy[1, x, PAD + 1 : PAD + 1 + ny, :]
            here3 = 3.0 * cy[1, x, mid, :] + cy[0, x, mid, :]
            low = slice(PAD - 1, PAD - 1 + ny)
            below3 = 3.0 * cy[1, x, low, :] + cy[0, x, low, :]
            below4 = cy[1, x, PAD - 2 : PAD - 2 + ny, :]
            kk[4, x] = below4
            kk[5, x] = -(below3 + below4)
            kk[6, x] = -(up4 + here3)
            kk[7, x] = up4
            centre = here3 + below3
            here4 = cz[1, x]
            here3 = 3.0 * here4 + cz[0, x]
            up4 = jnp.where(lanes < nz - 1, pltpu.roll(here4, nz - 1, 1), 0.0)
            below3 = jnp.where(lanes >= 1, pltpu.roll(here3, 1, 1), 0.0)
            below4 = jnp.where(lanes >= 2, pltpu.roll(here4, 2, 1), 0.0)
            kk[8, x] = below4
            kk[9, x] = jnp.where(lanes >= 1, -(below3 + below4), 0.0)
            kk[10, x] = jnp.where(lanes < nz - 1, -(up4 + here3), 0.0)
            kk[11, x] = jnp.where(lanes < nz - 2, up4, 0.0)
            kk[12, x] = centre + here3 + below3

    def stencil_layers():
        @pl.loop(0, lay)
        def _(x):
            up4 = cx[1, x + 3]
            here3 = 3.0 * cx[1, x + 2] + cx[0, x + 2]
            below3 = 3.0 * cx[1, x + 1] + cx[0, x + 1]
            below4 = cx[1, x]
            kk[0, x] = below4
            kk[1, x] = -(below3 + below4)
            kk[2, x] = -(up4 + here3)
            kk[3, x] = up4
            kk[12, x] += here3 + below3

    def send_layer(s, x):
        for i in range(per):
            send_out(s + 1, mirror(me // lay, i, per) * lay + x)

    def spatial(s, sending):
        factor = FACTORS[s]
        first, last = 2 * lo, lay - 2 * hi

        @pl.loop(0, lay)
        def _(i):
            x = back * (lay - 1 - i) + (1 - back) * i
            sums, central = [], [[], [], []]
            for b in range(nv):
                v0 = vp[s, b, x + 2, mid, :]
                total = kk[12, x] * v0 + gv[b, x]
                m2, m1 = vp[s, b, x, mid, :], vp[s, b, x + 1, mid, :]
                p1, p2 = vp[s, b, x + 3, mid, :], vp[s, b, x + 4, mid, :]
                total += kk[0, x] * m2 + kk[1, x] * m1 + kk[2, x] * p1 + kk[3, x] * p2
                central[0].append(m1 - p1)
                m2, m1, p1, p2 = (
                    vp[s, b, x + 2, PAD + o : PAD + o + ny, :] for o in (-2, -1, 1, 2)
                )
                total += kk[4, x] * m2 + kk[5, x] * m1 + kk[6, x] * p1 + kk[7, x] * p2
                central[1].append(m1 - p1)
                m2, m1, p1, p2 = (pltpu.roll(v0, o, 1) for o in (2, 1, nz - 1, nz - 2))
                total += kk[8, x] * m2 + kk[9, x] * m1 + kk[10, x] * p1 + kk[11, x] * p2
                central[2].append(keep_lo * m1 - keep_hi * p1)
                sums.append(total)
            step = factor * dtv[x]
            for b in range(nv):
                flux = jv[0, 0, b, x] * central[0][0]
                for d in range(3):
                    for a in range(nv):
                        if d or a:
                            flux += jv[d, a, b, x] * central[d][a]
                uh[s, b, x] = vp[0, b, x + 2, mid, :] - step * (sums[b] + 0.5 * flux)

            if sending:
                @pl.when(jnp.logical_and(x >= first, x < last))
                def _():
                    send_layer(s, x)

        def edge(x, side, near, far, k_near, k_far, sign):
            step = factor * dtv[x]
            for b in range(nv):
                flux = jv[0, 0, b, x] * hb[s, side, 0, near]
                for a in range(1, nv):
                    flux += jv[0, a, b, x] * hb[s, side, a, near]
                total = kk[k_near, x] * hb[s, side, b, near] + kk[k_far, x] * hb[s, side, b, far]
                uh[s, b, x] -= step * (total + sign * flux)

        def rim(x, side, near, k_far):
            step = factor * dtv[x]
            for b in range(nv):
                uh[s, b, x] -= step * (kk[k_far, x] * hb[s, side, b, near])

        @pl.when(has_lo)
        def _():
            halo_up(s).wait_recv()
            edge(0, 0, 1, 0, 1, 0, 0.5)
            rim(1, 0, 1, 0)

        @pl.when(has_hi)
        def _():
            halo_down(s).wait_recv()
            edge(lay - 1, 1, 0, 1, 2, 3, -0.5)
            rim(lay - 2, 1, 0, 3)

        if sending:
            @pl.loop(0, lay)
            def _(x):
                @pl.when(jnp.logical_or(x < first, x >= last))
                def _():
                    send_layer(s, x)

    def home_step(s):
        factor = FACTORS[s - 1]
        ready = 2 * (1 - both) + lay * both

        @pl.loop(0, lay)
        def _(i):
            x = back * i + (1 - back) * (lay - 1 - i)
            wait_bytes(mh.at[s - 1, :, x], mrs.at[s - 1, x])
            step = factor * dtv[x]
            for b in range(nv):
                vp[s, b, 2 + x, mid, :] = uh[s - 1, b, x] - step * mh[s - 1, b, x]

            @pl.when(i == ready - 1)
            def _():
                start_pair(halo_up(s), halo_down(s))

    def mix(s, value):
        @pl.loop(0, nv)
        def _(b):
            weights = [kv[i] for i in range(n)]
            turned = []
            for j in range(groups):
                v = value(b, slice(j * TILE, (j + 1) * TILE))
                turned.append([v] + [pltpu.roll(v, TILE - r * rows, 0) for r in range(1, pack)])
            for k in range(groups):
                total = None
                for j in range(groups):
                    for r in range(pack):
                        term = weights[(j - k) % groups * pack + r] * turned[j][r]
                        total = term if total is None else total + term
                mt[s, b, k * TILE : (k + 1) * TILE, :] = total

        send_home(s)

    def owner_start():
        wait_bytes(tb.at[0, 0:nv], trs.at[0])
        mix(0, lambda b, r: tb[0, b, r, :])

    def owner_step(s):
        wait_bytes(tb.at[s, 0 : width(s)], trs.at[s])
        factor = FACTORS[s - 1]
        mix(s, lambda b, r: tb[s, b, r, :] - factor * (tb[1, nv, r, :] * mt[s - 1, b, r, :]))

    slope, curve = coupling_tables(n)
    part = lax.broadcasted_iota(jnp.int32, (TILE, nz), 0) // rows
    local[10].wait()
    local[11].wait()
    for j in range(groups):
        for r in range(pack):
            rise = jnp.zeros((TILE, nz), jnp.float32)
            bend = jnp.zeros((TILE, nz), jnp.float32)
            for h in range(pack):
                m = (j * pack + (h + r) % pack - h) % n
                rise = jnp.where(part == h, slope[m], rise)
                bend = jnp.where(part == h, curve[m], bend)
            kv[j * pack + r] = freq[0] * rise + damp[0] * bend
    for s in range(SECTIONS):
        vp[s, :, 2 : 2 + lay, 0:PAD, :] = jnp.zeros((nv, lay, PAD, nz), jnp.float32)
        vp[s, :, 2 : 2 + lay, PAD + ny :, :] = jnp.zeros((nv, lay, PAD, nz), jnp.float32)
        vp[s, :, 0:2, mid, :] = jnp.zeros((nv, 2, ny, nz), jnp.float32)
        vp[s, :, 2 + lay :, mid, :] = jnp.zeros((nv, 2, ny, nz), jnp.float32)
    cy[:, :, 0:PAD, :] = jnp.zeros((2, lay, PAD, nz), jnp.float32)
    cy[:, :, PAD + ny :, :] = jnp.zeros((2, lay, PAD, nz), jnp.float32)

    @pl.when(jnp.logical_not(has_lo))
    def _():
        cx[:, 0:2] = jnp.zeros((2, 2, ny, nz), jnp.float32)

    @pl.when(jnp.logical_not(has_hi))
    def _():
        cx[:, 2 + lay :] = jnp.zeros((2, 2, ny, nz), jnp.float32)

    local[0].wait()
    local[2].wait()
    local[3].wait()
    pl.semaphore_wait(barrier, n - 1 + lo + hi)

    @pl.loop(0, n)
    def _(i):
        send_out(0, mirror(me, i, n))

    start_pair(coef_up, coef_down)
    start_pair(halo_up(0), halo_down(0))
    for c in [local[1]] + local[4:10]:
        c.wait()
    stencil_plane()
    land_pair(coef_up, coef_down)
    stencil_layers()
    spatial(0, True)
    owner_start()
    owner_step(1)
    home_step(1)
    spatial(1, True)
    home_step(2)
    spatial(2, True)
    owner_step(2)
    owner_step(3)
    home_step(3)
    spatial(3, True)
    home_step(4)
    spatial(4, False)
    owner_step(4)

    @pl.loop(0, lay)
    def _(x):
        wait_bytes(mh.at[4, :, x], mrs.at[4, x])
        step = FACTORS[4] * dtv[x]
        for b in range(nv):
            out[b, x] = uh[4, b, x] - step * mh[4, b, x]

    for unit in range(SECTIONS):
        wait_bytes(tb.at[unit, 0 : width(unit), 0 : (n - 1) * rows, :], ss.at[unit])
        wait_bytes(mt.at[unit, :, 0 : (n - 1) * rows, :], ss.at[SECTIONS + unit])
    for s in range(SECTIONS):
        sent_pair(halo_up(s), halo_down(s))
    sent_pair(coef_up, coef_down)


def on_device(n, cells, adjoint, grad, jac, c2, c4, dt, freq, damp):
    nv, lay, ny, nz = adjoint.shape[1:]
    rows = lay * ny // n
    assert rows * n == lay * ny and ny % rows == 0 and lay >= 2
    assert TILE % rows == 0 and (n * rows) % TILE == 0
    f32 = jnp.float32
    anywhere = pl.BlockSpec(memory_space=pl.ANY)
    dma = pltpu.SemaphoreType.DMA
    tall = ny + 2 * PAD
    result = pl.pallas_call(
        functools.partial(kernel, n, cells),
        out_shape=jax.ShapeDtypeStruct(adjoint.shape[1:], f32),
        in_specs=[anywhere] * 8,
        out_specs=pl.BlockSpec(memory_space=pltpu.VMEM),
        scratch_shapes=[
            pltpu.VMEM((SECTIONS, nv, lay + 4, tall, nz), f32),
            pltpu.VMEM(jac.shape[1:], f32),
            pltpu.VMEM((2, lay + 4, ny, nz), f32),
            pltpu.VMEM((2, lay, tall, nz), f32),
            pltpu.VMEM((2, lay, ny, nz), f32),
            pltpu.VMEM((13, lay, ny, nz), f32),
            pltpu.VMEM((nv, lay, ny, nz), f32),
            pltpu.VMEM((SECTIONS, nv + 1, lay, ny, nz), f32),
            pltpu.VMEM((SECTIONS, nv, lay, ny, nz), f32),
            pltpu.VMEM((SECTIONS, nv + 1, n * rows, nz), f32),
            pltpu.VMEM((SECTIONS, nv, n * rows, nz), f32),
            pltpu.VMEM((SECTIONS, 2, nv, 2, ny, nz), f32),
            pltpu.VMEM((n, TILE, nz), f32),
            pltpu.SMEM((1,), f32),
            pltpu.SMEM((1,), f32),
            dma((12,)),
            dma((2 * SECTIONS,)),
            dma((SECTIONS,)),
            dma((SECTIONS, lay)),
            dma((SECTIONS, 2)),
            dma((SECTIONS, 2)),
            dma((2,)),
            dma((2,)),
        ],
        compiler_params=pltpu.CompilerParams(collective_id=0, has_side_effects=True),
    )(adjoint[0], grad[0], jac[0], c2[0], c4[0], dt[0], freq, damp)
    return result[None]


def solution(mesh):
    placed = (
        P("inst", None, "cells", None, None),
        P("inst", None, "cells", None, None),
        P("inst", None, None, None, "cells", None, None),
        P("inst", None, "cells", None, None),
        P("inst", None, "cells", None, None),
        P("inst", "cells", None, None),
        P(),
        P(),
    )
    return jax.shard_map(
        functools.partial(on_device, mesh.shape["inst"], mesh.shape["cells"]),
        mesh=mesh,
        in_specs=placed,
        out_specs=P("inst", None, "cells", None, None),
        check_vma=False,
    )
```

```python
import functools
import math

import jax
import jax.numpy as jnp
from jax import lax
from jax.experimental import pallas as pl
from jax.experimental.pallas import tpu as pltpu
from jax.sharding import PartitionSpec as P

FACTORS = (0.25, 1.0 / 6.0, 0.375, 0.5, 1.0)
SECTIONS = len(FACTORS)
PAD = 8
TILE = 8
MESH = pl.DeviceIdType.MESH


def coupling_tables(count):
    slope, curve = [0.0], [count * count / 12.0 + 1.0 / 6.0]
    for m in range(1, count):
        parity = 1.0 if m % 2 == 0 else -1.0
        angle = math.pi * m / count
        slope.append(0.5 * parity * math.cos(angle) / math.sin(angle))
        curve.append(0.5 * parity / math.sin(angle) ** 2)
    return slope, curve


def kernel(
    n, cells, adj, grad, jac, c2, c4, dt, freq_in, damp_in, out,
    vp, jv, cx, cy, cz, kk, gv, uh, mh, tb, mt, hb, kv, freq, damp,
    loc_sem, ss, trs, mrs, hss, hrs, chs, chr_,
):
    nv, lay, ny, nz = adj.shape
    rows = lay * ny // n
    per = ny // rows
    pack = TILE // rows
    groups = n // pack
    me = lax.axis_index("inst")
    cell = lax.axis_index("cells")
    has_lo = cell > 0
    has_hi = cell < cells - 1
    lo = has_lo.astype(jnp.int32)
    hi = has_hi.astype(jnp.int32)
    both = lo * hi
    back = lo * (1 - both)
    mid = slice(PAD, PAD + ny)

    def mirrors(value, count):
        if count & (count - 1):
            return [lax.rem(value + i, count) for i in range(1, count)]
        moves, bit = [], 1
        while bit < count:
            moves.append((bit, bit - 2 * bit * lax.rem(lax.div(value, bit), 2)))
            bit *= 2
        found = []
        for flip in range(count - 1, 0, -1):
            other = value
            for bit, move in moves:
                if flip & bit:
                    other = other + move
            found.append(other)
        return found

    def spot(p):
        q = lax.div(p, lay)
        return lax.rem(p + q, lay), pl.multiple_of(q * rows, rows)

    others = mirrors(me, n)
    spots = [spot(p) for p in others]
    home_x, home_y = spot(me)
    own_q = lax.div(me, lay)
    turns = mirrors(own_q, per) + [own_q]

    barrier = pltpu.get_barrier_semaphore()

    for p in others:
        pl.semaphore_signal(barrier, inc=1, device_id={"inst": p}, device_id_type=MESH)

    @pl.when(has_lo)
    def _():
        pl.semaphore_signal(barrier, inc=1, device_id={"cells": cell - 1}, device_id_type=MESH)

    @pl.when(has_hi)
    def _():
        pl.semaphore_signal(barrier, inc=1, device_id={"cells": cell + 1}, device_id_type=MESH)

    local = [
        (adj, vp.at[0, :, 2 : 2 + lay, mid, :]),
        (dt, uh.at[0, nv]),
        (c2.at[0], cx.at[0, 2 : 2 + lay]),
        (c4.at[0], cx.at[1, 2 : 2 + lay]),
        (c2.at[1], cy.at[0, :, mid, :]),
        (c4.at[1], cy.at[1, :, mid, :]),
        (c2.at[2], cz.at[0]),
        (c4.at[2], cz.at[1]),
        (grad, gv),
        (jac, jv),
        (freq_in, freq),
        (damp_in, damp),
    ]
    local = [pltpu.make_async_copy(s, d, loc_sem.at[i]) for i, (s, d) in enumerate(local)]
    for c in local:
        c.start()
    dtv = uh.at[0, nv]

    def wait_bytes(ref, sem):
        pltpu.make_async_copy(ref, ref, sem).wait()

    def width(unit):
        return nv + 1 if unit == 1 else nv

    def owner_rows(p):
        return pl.ds(pl.multiple_of(p * rows, rows), rows)

    def chunk_at(unit, x, y):
        if unit == 0:
            return vp.at[0, :, 2 + x, pl.ds(pl.multiple_of(PAD + y, rows), rows), :]
        return uh.at[unit - 1, 0 : width(unit), x, pl.ds(y, rows), :]

    def send_out(unit, p, x, y):
        pltpu.make_async_remote_copy(
            src_ref=chunk_at(unit, x, y), dst_ref=tb.at[unit, 0 : width(unit), owner_rows(me), :],
            send_sem=ss.at[unit], recv_sem=trs.at[unit],
            device_id={"inst": p}, device_id_type=MESH,
        ).start()

    def keep_out(unit):
        pltpu.make_async_copy(
            chunk_at(unit, home_x, home_y), tb.at[unit, 0 : width(unit), owner_rows(me), :],
            trs.at[unit],
        ).start()

    def send_home(s):
        dst = mh.at[s, :, home_x, pl.ds(home_y, rows), :]
        for p in others:
            pltpu.make_async_remote_copy(
                src_ref=mt.at[s, :, owner_rows(p), :], dst_ref=dst,
                send_sem=ss.at[SECTIONS + s], recv_sem=mrs.at[s, home_x],
                device_id={"inst": p}, device_id_type=MESH,
            ).start()
        pltpu.make_async_copy(mt.at[s, :, owner_rows(me), :], dst, mrs.at[s, home_x]).start()

    def halo_up(s):
        return pltpu.make_async_remote_copy(
            src_ref=vp.at[s, :, lay : lay + 2, mid, :], dst_ref=hb.at[s, 0],
            send_sem=hss.at[s, 0], recv_sem=hrs.at[s, 0],
            device_id={"cells": cell + 1}, device_id_type=MESH,
        )

    def halo_down(s):
        return pltpu.make_async_remote_copy(
            src_ref=vp.at[s, :, 2:4, mid, :], dst_ref=hb.at[s, 1],
            send_sem=hss.at[s, 1], recv_sem=hrs.at[s, 1],
            device_id={"cells": cell - 1}, device_id_type=MESH,
        )

    coef_up = pltpu.make_async_remote_copy(
        src_ref=cx.at[:, lay : lay + 2], dst_ref=cx.at[:, 0:2],
        send_sem=chs.at[0], recv_sem=chr_.at[0],
        device_id={"cells": cell + 1}, device_id_type=MESH,
    )
    coef_down = pltpu.make_async_remote_copy(
        src_ref=cx.at[:, 2:4], dst_ref=cx.at[:, 2 + lay : 4 + lay],
        send_sem=chs.at[1], recv_sem=chr_.at[1],
        device_id={"cells": cell - 1}, device_id_type=MESH,
    )

    def start_pair(up, down):
        @pl.when(has_hi)
        def _():
            up.start()

        @pl.when(has_lo)
        def _():
            down.start()

    def land_pair(up, down):
        @pl.when(has_lo)
        def _():
            up.wait_recv()

        @pl.when(has_hi)
        def _():
            down.wait_recv()

    def sent_pair(up, down):
        @pl.when(has_hi)
        def _():
            up.wait_send()

        @pl.when(has_lo)
        def _():
            down.wait_send()

    lanes = lax.broadcasted_iota(jnp.int32, (ny, nz), 1)
    keep_lo = jnp.where(lanes >= 1, 1.0, 0.0)
    keep_hi = jnp.where(lanes < nz - 1, 1.0, 0.0)

    def stencil_plane():
        @pl.loop(0, lay)
        def _(x):
            up4 = cy[1, x, PAD + 1 : PAD + 1 + ny, :]
            here3 = 3.0 * cy[1, x, mid, :] + cy[0, x, mid, :]
            low = slice(PAD - 1, PAD - 1 + ny)
            below3 = 3.0 * cy[1, x, low, :] + cy[0, x, low, :]
            below4 = cy[1, x, PAD - 2 : PAD - 2 + ny, :]
            kk[4, x] = below4
            kk[5, x] = -(below3 + below4)
            kk[6, x] = -(up4 + here3)
            kk[7, x] = up4
            centre = here3 + below3
            here4 = cz[1, x]
            here3 = 3.0 * here4 + cz[0, x]
            up4 = jnp.where(lanes < nz - 1, pltpu.roll(here4, nz - 1, 1), 0.0)
            below3 = jnp.where(lanes >= 1, pltpu.roll(here3, 1, 1), 0.0)
            below4 = jnp.where(lanes >= 2, pltpu.roll(here4, 2, 1), 0.0)
            kk[8, x] = below4
            kk[9, x] = jnp.where(lanes >= 1, -(below3 + below4), 0.0)
            kk[10, x] = jnp.where(lanes < nz - 1, -(up4 + here3), 0.0)
            kk[11, x] = jnp.where(lanes < nz - 2, up4, 0.0)
            kk[12, x] = centre + here3 + below3

    def stencil_layers():
        @pl.loop(0, lay)
        def _(x):
            up4 = cx[1, x + 3]
            here3 = 3.0 * cx[1, x + 2] + cx[0, x + 2]
            below3 = 3.0 * cx[1, x + 1] + cx[0, x + 1]
            below4 = cx[1, x]
            kk[0, x] = below4
            kk[1, x] = -(below3 + below4)
            kk[2, x] = -(up4 + here3)
            kk[3, x] = up4
            kk[12, x] += here3 + below3

    def send_layer(s, x):
        for i, q in enumerate(turns):
            p = q * lay + lax.rem(x + (lay * per - q), lay)
            y = pl.multiple_of(q * rows, rows)
            if i < per - 1:
                send_out(s + 1, p, x, y)
            else:
                @pl.when(x != home_x)
                def _():
                    send_out(s + 1, p, x, y)

                @pl.when(x == home_x)
                def _():
                    keep_out(s + 1)

    def spatial(s, sending):
        factor = FACTORS[s]
        first, last = 2 * lo, lay - 2 * hi

        @pl.loop(0, lay)
        def _(i):
            x = back * (lay - 1 - i) + (1 - back) * i
            sums, central = [], [[], [], []]
            for b in range(nv):
                v0 = vp[s, b, x + 2, mid, :]
                total = kk[12, x] * v0 + gv[b, x]
                m2, m1 = vp[s, b, x, mid, :], vp[s, b, x + 1, mid, :]
                p1, p2 = vp[s, b, x + 3, mid, :], vp[s, b, x + 4, mid, :]
                total += kk[0, x] * m2 + kk[1, x] * m1 + kk[2, x] * p1 + kk[3, x] * p2
                central[0].append(m1 - p1)
                m2, m1, p1, p2 = (
                    vp[s, b, x + 2, PAD + o : PAD + o + ny, :] for o in (-2, -1, 1, 2)
                )
                total += kk[4, x] * m2 + kk[5, x] * m1 + kk[6, x] * p1 + kk[7, x] * p2
                central[1].append(m1 - p1)
                m2, m1, p1, p2 = (pltpu.roll(v0, o, 1) for o in (2, 1, nz - 1, nz - 2))
                total += kk[8, x] * m2 + kk[9, x] * m1 + kk[10, x] * p1 + kk[11, x] * p2
                central[2].append(keep_lo * m1 - keep_hi * p1)
                sums.append(total)
            step = factor * dtv[x]
            for b in range(nv):
                flux = jv[0, 0, b, x] * central[0][0]
                for d in range(3):
                    for a in range(nv):
                        if d or a:
                            flux += jv[d, a, b, x] * central[d][a]
                uh[s, b, x] = vp[0, b, x + 2, mid, :] - step * (sums[b] + 0.5 * flux)

            if sending:
                @pl.when(jnp.logical_and(x >= first, x < last))
                def _():
                    send_layer(s, x)

        def edge(x, side, near, far, k_near, k_far, sign):
            step = factor * dtv[x]
            for b in range(nv):
                flux = jv[0, 0, b, x] * hb[s, side, 0, near]
                for a in range(1, nv):
                    flux += jv[0, a, b, x] * hb[s, side, a, near]
                total = kk[k_near, x] * hb[s, side, b, near] + kk[k_far, x] * hb[s, side, b, far]
                uh[s, b, x] -= step * (total + sign * flux)

        def rim(x, side, near, k_far):
            step = factor * dtv[x]
            for b in range(nv):
                uh[s, b, x] -= step * (kk[k_far, x] * hb[s, side, b, near])

        @pl.when(has_lo)
        def _():
            halo_up(s).wait_recv()
            edge(0, 0, 1, 0, 1, 0, 0.5)
            rim(1, 0, 1, 0)

        @pl.when(has_hi)
        def _():
            halo_down(s).wait_recv()
            edge(lay - 1, 1, 0, 1, 2, 3, -0.5)
            rim(lay - 2, 1, 0, 3)

        if sending:
            @pl.loop(0, lay)
            def _(x):
                @pl.when(jnp.logical_or(x < first, x >= last))
                def _():
                    send_layer(s, x)

    def home_step(s):
        factor = FACTORS[s - 1]
        ready = 2 * (1 - both) + lay * both

        @pl.loop(0, lay)
        def _(i):
            x = back * i + (1 - back) * (lay - 1 - i)
            wait_bytes(mh.at[s - 1, :, x], mrs.at[s - 1, x])
            step = factor * dtv[x]
            for b in range(nv):
                vp[s, b, 2 + x, mid, :] = uh[s - 1, b, x] - step * mh[s - 1, b, x]

            @pl.when(i == ready - 1)
            def _():
                start_pair(halo_up(s), halo_down(s))

    def mix(s, value):
        @pl.loop(0, nv)
        def _(b):
            weights = [kv[i] for i in range(n)]
            turned = []
            for j in range(groups):
                v = value(b, slice(j * TILE, (j + 1) * TILE))
                turned.append([v] + [pltpu.roll(v, TILE - r * rows, 0) for r in range(1, pack)])
            for k in range(groups):
                total = None
                for j in range(groups):
                    for r in range(pack):
                        term = weights[(j - k) % groups * pack + r] * turned[j][r]
                        total = term if total is None else total + term
                mt[s, b, k * TILE : (k + 1) * TILE, :] = total

        send_home(s)

    def owner_start():
        wait_bytes(tb.at[0, 0:nv], trs.at[0])
        mix(0, lambda b, r: tb[0, b, r, :])

    def owner_step(s):
        wait_bytes(tb.at[s, 0 : width(s)], trs.at[s])
        factor = FACTORS[s - 1]
        mix(s, lambda b, r: tb[s, b, r, :] - factor * (tb[1, nv, r, :] * mt[s - 1, b, r, :]))

    slope, curve = coupling_tables(n)
    part = lax.broadcasted_iota(jnp.int32, (TILE, nz), 0) // rows
    local[10].wait()
    local[11].wait()
    for j in range(groups):
        for r in range(pack):
            rise = jnp.zeros((TILE, nz), jnp.float32)
            bend = jnp.zeros((TILE, nz), jnp.float32)
            for h in range(pack):
                m = (j * pack + (h + r) % pack - h) % n
                rise = jnp.where(part == h, slope[m], rise)
                bend = jnp.where(part == h, curve[m], bend)
            kv[j * pack + r] = freq[0] * rise + damp[0] * bend
    for s in range(SECTIONS):
        vp[s, :, 2 : 2 + lay, 0:PAD, :] = jnp.zeros((nv, lay, PAD, nz), jnp.float32)
        vp[s, :, 2 : 2 + lay, PAD + ny :, :] = jnp.zeros((nv, lay, PAD, nz), jnp.float32)
        vp[s, :, 0:2, mid, :] = jnp.zeros((nv, 2, ny, nz), jnp.float32)
        vp[s, :, 2 + lay :, mid, :] = jnp.zeros((nv, 2, ny, nz), jnp.float32)
    cy[:, :, 0:PAD, :] = jnp.zeros((2, lay, PAD, nz), jnp.float32)
    cy[:, :, PAD + ny :, :] = jnp.zeros((2, lay, PAD, nz), jnp.float32)

    @pl.when(jnp.logical_not(has_lo))
    def _():
        cx[:, 0:2] = jnp.zeros((2, 2, ny, nz), jnp.float32)

    @pl.when(jnp.logical_not(has_hi))
    def _():
        cx[:, 2 + lay :] = jnp.zeros((2, 2, ny, nz), jnp.float32)

    local[0].wait()
    local[2].wait()
    local[3].wait()
    pl.semaphore_wait(barrier, n - 1 + lo + hi)

    for p, (x, y) in zip(others, spots):
        send_out(0, p, x, y)
    keep_out(0)
    start_pair(coef_up, coef_down)
    start_pair(halo_up(0), halo_down(0))
    for c in [local[1]] + local[4:10]:
        c.wait()
    stencil_plane()
    land_pair(coef_up, coef_down)
    stencil_layers()
    spatial(0, True)
    owner_start()
    owner_step(1)
    home_step(1)
    spatial(1, True)
    home_step(2)
    spatial(2, True)
    owner_step(2)
    owner_step(3)
    home_step(3)
    spatial(3, True)
    home_step(4)
    spatial(4, False)
    owner_step(4)

    @pl.loop(0, lay)
    def _(x):
        wait_bytes(mh.at[4, :, x], mrs.at[4, x])
        step = FACTORS[4] * dtv[x]
        for b in range(nv):
            out[b, x] = uh[4, b, x] - step * mh[4, b, x]

    for unit in range(SECTIONS):
        wait_bytes(tb.at[unit, 0 : width(unit), 0 : (n - 1) * rows, :], ss.at[unit])
        wait_bytes(mt.at[unit, :, 0 : (n - 1) * rows, :], ss.at[SECTIONS + unit])
    for s in range(SECTIONS):
        sent_pair(halo_up(s), halo_down(s))
    sent_pair(coef_up, coef_down)


def on_device(n, cells, adjoint, grad, jac, c2, c4, dt, freq, damp):
    nv, lay, ny, nz = adjoint.shape[1:]
    rows = lay * ny // n
    assert rows * n == lay * ny and ny % rows == 0 and lay >= 2
    assert TILE % rows == 0 and (n * rows) % TILE == 0
    f32 = jnp.float32
    anywhere = pl.BlockSpec(memory_space=pl.ANY)
    dma = pltpu.SemaphoreType.DMA
    tall = ny + 2 * PAD
    result = pl.pallas_call(
        functools.partial(kernel, n, cells),
        out_shape=jax.ShapeDtypeStruct(adjoint.shape[1:], f32),
        in_specs=[anywhere] * 8,
        out_specs=pl.BlockSpec(memory_space=pltpu.VMEM),
        scratch_shapes=[
            pltpu.VMEM((SECTIONS, nv, lay + 4, tall, nz), f32),
            pltpu.VMEM(jac.shape[1:], f32),
            pltpu.VMEM((2, lay + 4, ny, nz), f32),
            pltpu.VMEM((2, lay, tall, nz), f32),
            pltpu.VMEM((2, lay, ny, nz), f32),
            pltpu.VMEM((13, lay, ny, nz), f32),
            pltpu.VMEM((nv, lay, ny, nz), f32),
            pltpu.VMEM((SECTIONS, nv + 1, lay, ny, nz), f32),
            pltpu.VMEM((SECTIONS, nv, lay, ny, nz), f32),
            pltpu.VMEM((SECTIONS, nv + 1, n * rows, nz), f32),
            pltpu.VMEM((SECTIONS, nv, n * rows, nz), f32),
            pltpu.VMEM((SECTIONS, 2, nv, 2, ny, nz), f32),
            pltpu.VMEM((n, TILE, nz), f32),
            pltpu.SMEM((1,), f32),
            pltpu.SMEM((1,), f32),
            dma((12,)),
            dma((2 * SECTIONS,)),
            dma((SECTIONS,)),
            dma((SECTIONS, lay)),
            dma((SECTIONS, 2)),
            dma((SECTIONS, 2)),
            dma((2,)),
            dma((2,)),
        ],
        compiler_params=pltpu.CompilerParams(collective_id=0, has_side_effects=True),
    )(adjoint[0], grad[0], jac[0], c2[0], c4[0], dt[0], freq, damp)
    return result[None]


def solution(mesh):
    placed = (
        P("inst", None, "cells", None, None),
        P("inst", None, "cells", None, None),
        P("inst", None, None, None, "cells", None, None),
        P("inst", None, "cells", None, None),
        P("inst", None, "cells", None, None),
        P("inst", "cells", None, None),
        P(),
        P(),
    )
    return jax.shard_map(
        functools.partial(on_device, mesh.shape["inst"], mesh.shape["cells"]),
        mesh=mesh,
        in_specs=placed,
        out_specs=P("inst", None, "cells", None, None),
        check_vma=False,
    )
```

```python
import functools
import math

import jax
import jax.numpy as jnp
from jax import lax
from jax.experimental import pallas as pl
from jax.experimental.pallas import tpu as pltpu
from jax.sharding import PartitionSpec as P

FACTORS = (0.25, 1.0 / 6.0, 0.375, 0.5, 1.0)
SECTIONS = len(FACTORS)
PAD = 8
TILE = 8
MESH = pl.DeviceIdType.MESH


def coupling_tables(count):
    slope, curve = [0.0], [count * count / 12.0 + 1.0 / 6.0]
    for m in range(1, count):
        parity = 1.0 if m % 2 == 0 else -1.0
        angle = math.pi * m / count
        slope.append(0.5 * parity * math.cos(angle) / math.sin(angle))
        curve.append(0.5 * parity / math.sin(angle) ** 2)
    return slope, curve


def kernel(
    n, cells, adj, grad, jac, c2, c4, dt, freq_in, damp_in, out,
    vp, jv, cx, cy, cz, kk, gv, uh, mh, tb, mt, hb, kv, freq, damp,
    loc_sem, ss, trs, mrs, hss, hrs, chs, chr_,
):
    nv, lay, ny, nz = adj.shape
    rows = lay * ny // n
    per = ny // rows
    pack = TILE // rows
    groups = n // pack
    me = lax.axis_index("inst")
    cell = lax.axis_index("cells")
    has_lo = cell > 0
    has_hi = cell < cells - 1
    lo = has_lo.astype(jnp.int32)
    hi = has_hi.astype(jnp.int32)
    both = lo * hi
    back = lo * (1 - both)
    mid = slice(PAD, PAD + ny)

    def mirrors(value, count):
        if count & (count - 1):
            return [lax.rem(value + i, count) for i in range(1, count)]
        moves, bit = [], 1
        while bit < count:
            moves.append((bit, bit - 2 * bit * lax.rem(lax.div(value, bit), 2)))
            bit *= 2
        found = []
        for flip in range(count - 1, 0, -1):
            other = value
            for bit, move in moves:
                if flip & bit:
                    other = other + move
            found.append(other)
        return found

    def spot(p):
        q = lax.div(p, lay)
        return lax.rem(p + q, lay), pl.multiple_of(q * rows, rows)

    others = mirrors(me, n)
    spots = [spot(p) for p in others]
    home_x, home_y = spot(me)
    own_q = lax.div(me, lay)
    turns = mirrors(own_q, per) + [own_q]

    barrier = pltpu.get_barrier_semaphore()

    for p in others:
        pl.semaphore_signal(barrier, inc=1, device_id={"inst": p}, device_id_type=MESH)

    @pl.when(has_lo)
    def _():
        pl.semaphore_signal(barrier, inc=1, device_id={"cells": cell - 1}, device_id_type=MESH)

    @pl.when(has_hi)
    def _():
        pl.semaphore_signal(barrier, inc=1, device_id={"cells": cell + 1}, device_id_type=MESH)

    local = [
        (adj, vp.at[0, :, 2 : 2 + lay, mid, :]),
        (dt, uh.at[0, nv]),
        (c2.at[0], cx.at[0, 2 : 2 + lay]),
        (c4.at[0], cx.at[1, 2 : 2 + lay]),
        (c2.at[1], cy.at[0, :, mid, :]),
        (c4.at[1], cy.at[1, :, mid, :]),
        (c2.at[2], cz.at[0]),
        (c4.at[2], cz.at[1]),
        (grad, gv),
        (jac, jv),
        (freq_in, freq),
        (damp_in, damp),
    ]
    local = [pltpu.make_async_copy(s, d, loc_sem.at[i]) for i, (s, d) in enumerate(local)]
    for c in local:
        c.start()
    dtv = uh.at[0, nv]

    def wait_bytes(ref, sem):
        pltpu.make_async_copy(ref, ref, sem).wait()

    def width(unit):
        return nv + 1 if unit == 1 else nv

    def owner_rows(p):
        return pl.ds(pl.multiple_of(p * rows, rows), rows)

    def chunk_at(unit, x, y):
        if unit == 0:
            return vp.at[0, :, 2 + x, pl.ds(pl.multiple_of(PAD + y, rows), rows), :]
        return uh.at[unit - 1, 0 : width(unit), x, pl.ds(y, rows), :]

    def send_out(unit, p, x, y):
        pltpu.make_async_remote_copy(
            src_ref=chunk_at(unit, x, y), dst_ref=tb.at[unit, 0 : width(unit), owner_rows(me), :],
            send_sem=ss.at[unit], recv_sem=trs.at[unit],
            device_id={"inst": p}, device_id_type=MESH,
        ).start()

    def keep_out(unit):
        pltpu.make_async_copy(
            chunk_at(unit, home_x, home_y), tb.at[unit, 0 : width(unit), owner_rows(me), :],
            trs.at[unit],
        ).start()

    def send_home(s):
        dst = mh.at[s, :, home_x, pl.ds(home_y, rows), :]
        for p in others:
            pltpu.make_async_remote_copy(
                src_ref=mt.at[s, :, owner_rows(p), :], dst_ref=dst,
                send_sem=ss.at[SECTIONS + s], recv_sem=mrs.at[s, home_x],
                device_id={"inst": p}, device_id_type=MESH,
            ).start()
        pltpu.make_async_copy(mt.at[s, :, owner_rows(me), :], dst, mrs.at[s, home_x]).start()

    def halo_up(s):
        return pltpu.make_async_remote_copy(
            src_ref=vp.at[s, :, lay : lay + 2, mid, :], dst_ref=hb.at[s, 0],
            send_sem=hss.at[s, 0], recv_sem=hrs.at[s, 0],
            device_id={"cells": cell + 1}, device_id_type=MESH,
        )

    def halo_down(s):
        return pltpu.make_async_remote_copy(
            src_ref=vp.at[s, :, 2:4, mid, :], dst_ref=hb.at[s, 1],
            send_sem=hss.at[s, 1], recv_sem=hrs.at[s, 1],
            device_id={"cells": cell - 1}, device_id_type=MESH,
        )

    coef_up = pltpu.make_async_remote_copy(
        src_ref=cx.at[:, lay : lay + 2], dst_ref=cx.at[:, 0:2],
        send_sem=chs.at[0], recv_sem=chr_.at[0],
        device_id={"cells": cell + 1}, device_id_type=MESH,
    )
    coef_down = pltpu.make_async_remote_copy(
        src_ref=cx.at[:, 2:4], dst_ref=cx.at[:, 2 + lay : 4 + lay],
        send_sem=chs.at[1], recv_sem=chr_.at[1],
        device_id={"cells": cell - 1}, device_id_type=MESH,
    )

    def start_pair(up, down):
        @pl.when(has_hi)
        def _():
            up.start()

        @pl.when(has_lo)
        def _():
            down.start()

    def land_pair(up, down):
        @pl.when(has_lo)
        def _():
            up.wait_recv()

        @pl.when(has_hi)
        def _():
            down.wait_recv()

    def sent_pair(up, down):
        @pl.when(has_hi)
        def _():
            up.wait_send()

        @pl.when(has_lo)
        def _():
            down.wait_send()

    lanes = lax.broadcasted_iota(jnp.int32, (ny, nz), 1)
    keep_lo = jnp.where(lanes >= 1, 1.0, 0.0)
    keep_hi = jnp.where(lanes < nz - 1, 1.0, 0.0)

    def stencil_plane():
        @pl.loop(0, lay)
        def _(x):
            up4 = cy[1, x, PAD + 1 : PAD + 1 + ny, :]
            here3 = 3.0 * cy[1, x, mid, :] + cy[0, x, mid, :]
            low = slice(PAD - 1, PAD - 1 + ny)
            below3 = 3.0 * cy[1, x, low, :] + cy[0, x, low, :]
            below4 = cy[1, x, PAD - 2 : PAD - 2 + ny, :]
            kk[4, x] = below4
            kk[5, x] = -(below3 + below4)
            kk[6, x] = -(up4 + here3)
            kk[7, x] = up4
            centre = here3 + below3
            here4 = cz[1, x]
            here3 = 3.0 * here4 + cz[0, x]
            up4 = jnp.where(lanes < nz - 1, pltpu.roll(here4, nz - 1, 1), 0.0)
            below3 = jnp.where(lanes >= 1, pltpu.roll(here3, 1, 1), 0.0)
            below4 = jnp.where(lanes >= 2, pltpu.roll(here4, 2, 1), 0.0)
            kk[8, x] = below4
            kk[9, x] = jnp.where(lanes >= 1, -(below3 + below4), 0.0)
            kk[10, x] = jnp.where(lanes < nz - 1, -(up4 + here3), 0.0)
            kk[11, x] = jnp.where(lanes < nz - 2, up4, 0.0)
            kk[12, x] = centre + here3 + below3

    def stencil_layers():
        @pl.loop(0, lay)
        def _(x):
            up4 = cx[1, x + 3]
            here3 = 3.0 * cx[1, x + 2] + cx[0, x + 2]
            below3 = 3.0 * cx[1, x + 1] + cx[0, x + 1]
            below4 = cx[1, x]
            kk[0, x] = below4
            kk[1, x] = -(below3 + below4)
            kk[2, x] = -(up4 + here3)
            kk[3, x] = up4
            kk[12, x] += here3 + below3

    def send_layer(s, x):
        for i, q in enumerate(turns):
            p = q * lay + lax.rem(x + (lay * per - q), lay)
            y = pl.multiple_of(q * rows, rows)
            if i < per - 1:
                send_out(s + 1, p, x, y)
            else:
                @pl.when(x != home_x)
                def _():
                    send_out(s + 1, p, x, y)

                @pl.when(x == home_x)
                def _():
                    keep_out(s + 1)

    def spatial(s, sending):
        factor = FACTORS[s]
        first, last = 2 * lo, lay - 2 * hi

        @pl.loop(0, lay)
        def _(i):
            x = back * (lay - 1 - i) + (1 - back) * i
            sums, central = [], [[], [], []]
            for b in range(nv):
                v0 = vp[s, b, x + 2, mid, :]
                total = kk[12, x] * v0 + gv[b, x]
                m2, m1 = vp[s, b, x, mid, :], vp[s, b, x + 1, mid, :]
                p1, p2 = vp[s, b, x + 3, mid, :], vp[s, b, x + 4, mid, :]
                total += kk[0, x] * m2 + kk[1, x] * m1 + kk[2, x] * p1 + kk[3, x] * p2
                central[0].append(m1 - p1)
                m2, m1, p1, p2 = (
                    vp[s, b, x + 2, PAD + o : PAD + o + ny, :] for o in (-2, -1, 1, 2)
                )
                total += kk[4, x] * m2 + kk[5, x] * m1 + kk[6, x] * p1 + kk[7, x] * p2
                central[1].append(m1 - p1)
                m2, m1, p1, p2 = (pltpu.roll(v0, o, 1) for o in (2, 1, nz - 1, nz - 2))
                total += kk[8, x] * m2 + kk[9, x] * m1 + kk[10, x] * p1 + kk[11, x] * p2
                central[2].append(keep_lo * m1 - keep_hi * p1)
                sums.append(total)
            step = factor * dtv[x]
            for b in range(nv):
                flux = jv[0, 0, b, x] * central[0][0]
                for d in range(3):
                    for a in range(nv):
                        if d or a:
                            flux += jv[d, a, b, x] * central[d][a]
                uh[s, b, x] = vp[0, b, x + 2, mid, :] - step * (sums[b] + 0.5 * flux)

            if sending:
                @pl.when(jnp.logical_and(x >= first, x < last))
                def _():
                    send_layer(s, x)

        def edge(x, side, near, far, k_near, k_far, sign):
            step = factor * dtv[x]
            for b in range(nv):
                flux = jv[0, 0, b, x] * hb[s, side, 0, near]
                for a in range(1, nv):
                    flux += jv[0, a, b, x] * hb[s, side, a, near]
                total = kk[k_near, x] * hb[s, side, b, near] + kk[k_far, x] * hb[s, side, b, far]
                uh[s, b, x] -= step * (total + sign * flux)

        def rim(x, side, near, k_far):
            step = factor * dtv[x]
            for b in range(nv):
                uh[s, b, x] -= step * (kk[k_far, x] * hb[s, side, b, near])

        @pl.when(has_lo)
        def _():
            halo_up(s).wait_recv()
            edge(0, 0, 1, 0, 1, 0, 0.5)
            rim(1, 0, 1, 0)

        @pl.when(has_hi)
        def _():
            halo_down(s).wait_recv()
            edge(lay - 1, 1, 0, 1, 2, 3, -0.5)
            rim(lay - 2, 1, 0, 3)

        if sending:
            @pl.loop(0, lay)
            def _(x):
                @pl.when(jnp.logical_or(x < first, x >= last))
                def _():
                    send_layer(s, x)

    def home_step(s):
        factor = FACTORS[s - 1]
        ready = 2 * (1 - both) + lay * both

        @pl.loop(0, lay)
        def _(i):
            x = back * i + (1 - back) * (lay - 1 - i)
            wait_bytes(mh.at[s - 1, :, x], mrs.at[s - 1, x])
            step = factor * dtv[x]
            for b in range(nv):
                vp[s, b, 2 + x, mid, :] = uh[s - 1, b, x] - step * mh[s - 1, b, x]

            @pl.when(i == ready - 1)
            def _():
                start_pair(halo_up(s), halo_down(s))

    def mix(s, value):
        @pl.loop(0, nv)
        def _(b):
            weights = [kv[i] for i in range(n)]
            turned = []
            for j in range(groups):
                v = value(b, slice(j * TILE, (j + 1) * TILE))
                turned.append([v] + [pltpu.roll(v, TILE - r * rows, 0) for r in range(1, pack)])
            for k in range(groups):
                total = None
                for j in range(groups):
                    for r in range(pack):
                        term = weights[(j - k) % groups * pack + r] * turned[j][r]
                        total = term if total is None else total + term
                mt[s, b, k * TILE : (k + 1) * TILE, :] = total

        send_home(s)

    def owner_start():
        wait_bytes(tb.at[0, 0:nv], trs.at[0])
        mix(0, lambda b, r: tb[0, b, r, :])

    def owner_step(s):
        wait_bytes(tb.at[s, 0 : width(s)], trs.at[s])
        factor = FACTORS[s - 1]
        mix(s, lambda b, r: tb[s, b, r, :] - factor * (tb[1, nv, r, :] * mt[s - 1, b, r, :]))

    slope, curve = coupling_tables(n)
    part = lax.broadcasted_iota(jnp.int32, (TILE, nz), 0) // rows
    local[10].wait()
    local[11].wait()
    for j in range(groups):
        for r in range(pack):
            rise = jnp.zeros((TILE, nz), jnp.float32)
            bend = jnp.zeros((TILE, nz), jnp.float32)
            for h in range(pack):
                m = (j * pack + (h + r) % pack - h) % n
                rise = jnp.where(part == h, slope[m], rise)
                bend = jnp.where(part == h, curve[m], bend)
            kv[j * pack + r] = freq[0] * rise + damp[0] * bend
    for s in range(SECTIONS):
        vp[s, :, 2 : 2 + lay, 0:PAD, :] = jnp.zeros((nv, lay, PAD, nz), jnp.float32)
        vp[s, :, 2 : 2 + lay, PAD + ny :, :] = jnp.zeros((nv, lay, PAD, nz), jnp.float32)
        vp[s, :, 0:2, mid, :] = jnp.zeros((nv, 2, ny, nz), jnp.float32)
        vp[s, :, 2 + lay :, mid, :] = jnp.zeros((nv, 2, ny, nz), jnp.float32)
    cy[:, :, 0:PAD, :] = jnp.zeros((2, lay, PAD, nz), jnp.float32)
    cy[:, :, PAD + ny :, :] = jnp.zeros((2, lay, PAD, nz), jnp.float32)

    @pl.when(jnp.logical_not(has_lo))
    def _():
        cx[:, 0:2] = jnp.zeros((2, 2, ny, nz), jnp.float32)

    @pl.when(jnp.logical_not(has_hi))
    def _():
        cx[:, 2 + lay :] = jnp.zeros((2, 2, ny, nz), jnp.float32)

    local[0].wait()
    local[2].wait()
    local[3].wait()
    pl.semaphore_wait(barrier, n - 1 + lo + hi)

    for p, (x, y) in zip(others, spots):
        send_out(0, p, x, y)
    keep_out(0)
    start_pair(coef_up, coef_down)
    start_pair(halo_up(0), halo_down(0))
    for c in [local[1]] + local[4:10]:
        c.wait()
    stencil_plane()
    land_pair(coef_up, coef_down)
    stencil_layers()
    spatial(0, True)
    owner_start()
    owner_step(1)
    home_step(1)
    spatial(1, True)
    home_step(2)
    spatial(2, True)
    owner_step(2)
    owner_step(3)
    home_step(3)
    spatial(3, True)
    home_step(4)
    spatial(4, False)
    owner_step(4)

    @pl.loop(0, lay)
    def _(x):
        wait_bytes(mh.at[4, :, x], mrs.at[4, x])
        step = FACTORS[4] * dtv[x]
        for b in range(nv):
            out[b, x] = uh[4, b, x] - step * mh[4, b, x]

    for unit in range(SECTIONS):
        wait_bytes(tb.at[unit, 0 : width(unit), 0 : (n - 1) * rows, :], ss.at[unit])
        wait_bytes(mt.at[unit, :, 0 : (n - 1) * rows, :], ss.at[SECTIONS + unit])
    for s in range(SECTIONS):
        sent_pair(halo_up(s), halo_down(s))
    sent_pair(coef_up, coef_down)


def on_device(n, cells, adjoint, grad, jac, c2, c4, dt, freq, damp):
    nv, lay, ny, nz = adjoint.shape[1:]
    rows = lay * ny // n
    assert rows * n == lay * ny and ny % rows == 0 and lay >= 2
    assert TILE % rows == 0 and (n * rows) % TILE == 0
    f32 = jnp.float32
    anywhere = pl.BlockSpec(memory_space=pl.ANY)
    dma = pltpu.SemaphoreType.DMA
    tall = ny + 2 * PAD
    result = pl.pallas_call(
        functools.partial(kernel, n, cells),
        out_shape=pltpu.VMEM(adjoint.shape[1:], f32),
        in_specs=[anywhere] * 8,
        out_specs=pl.BlockSpec(memory_space=pltpu.VMEM),
        scratch_shapes=[
            pltpu.VMEM((SECTIONS, nv, lay + 4, tall, nz), f32),
            pltpu.VMEM(jac.shape[1:], f32),
            pltpu.VMEM((2, lay + 4, ny, nz), f32),
            pltpu.VMEM((2, lay, tall, nz), f32),
            pltpu.VMEM((2, lay, ny, nz), f32),
            pltpu.VMEM((13, lay, ny, nz), f32),
            pltpu.VMEM((nv, lay, ny, nz), f32),
            pltpu.VMEM((SECTIONS, nv + 1, lay, ny, nz), f32),
            pltpu.VMEM((SECTIONS, nv, lay, ny, nz), f32),
            pltpu.VMEM((SECTIONS, nv + 1, n * rows, nz), f32),
            pltpu.VMEM((SECTIONS, nv, n * rows, nz), f32),
            pltpu.VMEM((SECTIONS, 2, nv, 2, ny, nz), f32),
            pltpu.VMEM((n, TILE, nz), f32),
            pltpu.SMEM((1,), f32),
            pltpu.SMEM((1,), f32),
            dma((12,)),
            dma((2 * SECTIONS,)),
            dma((SECTIONS,)),
            dma((SECTIONS, lay)),
            dma((SECTIONS, 2)),
            dma((SECTIONS, 2)),
            dma((2,)),
            dma((2,)),
        ],
        compiler_params=pltpu.CompilerParams(collective_id=0, has_side_effects=True),
    )(adjoint[0], grad[0], jac[0], c2[0], c4[0], dt[0], freq, damp)
    return result[None]


def solution(mesh):
    placed = (
        P("inst", None, "cells", None, None),
        P("inst", None, "cells", None, None),
        P("inst", None, None, None, "cells", None, None),
        P("inst", None, "cells", None, None),
        P("inst", None, "cells", None, None),
        P("inst", "cells", None, None),
        P(),
        P(),
    )
    return jax.shard_map(
        functools.partial(on_device, mesh.shape["inst"], mesh.shape["cells"]),
        mesh=mesh,
        in_specs=placed,
        out_specs=P("inst", None, "cells", None, None),
        check_vma=False,
    )
```

```python
import functools
import math

import jax
import jax.numpy as jnp
from jax import lax
from jax.experimental import pallas as pl
from jax.experimental.pallas import tpu as pltpu
from jax.sharding import PartitionSpec as P

FACTORS = (0.25, 1.0 / 6.0, 0.375, 0.5, 1.0)
SECTIONS = len(FACTORS)
PAD = 8
TILE = 8
MESH = pl.DeviceIdType.MESH


def coupling_tables(count):
    slope, curve = [0.0], [count * count / 12.0 + 1.0 / 6.0]
    for m in range(1, count):
        parity = 1.0 if m % 2 == 0 else -1.0
        angle = math.pi * m / count
        slope.append(0.5 * parity * math.cos(angle) / math.sin(angle))
        curve.append(0.5 * parity / math.sin(angle) ** 2)
    return slope, curve


def kernel(
    n, cells, adj, grad, jac, c2, c4, dt, freq_in, damp_in, out,
    vp, jv, cx, cy, cz, kk, gv, uh, mh, tb, mt, hb, kv, freq, damp,
    loc_sem, ss, trs, mrs, hss, hrs, chs, chr_,
):
    nv, lay, ny, nz = adj.shape
    rows = lay * ny // n
    per = ny // rows
    pack = TILE // rows
    groups = n // pack
    me = lax.axis_index("inst")
    cell = lax.axis_index("cells")
    has_lo = cell > 0
    has_hi = cell < cells - 1
    lo = has_lo.astype(jnp.int32)
    hi = has_hi.astype(jnp.int32)
    both = lo * hi
    back = lo * (1 - both)
    mid = slice(PAD, PAD + ny)

    def mirrors(value, count):
        if count & (count - 1):
            return [lax.rem(value + i, count) for i in range(1, count)]
        moves, bit = [], 1
        while bit < count:
            moves.append((bit, bit - 2 * bit * lax.rem(lax.div(value, bit), 2)))
            bit *= 2
        found = []
        for flip in range(count - 1, 0, -1):
            other = value
            for bit, move in moves:
                if flip & bit:
                    other = other + move
            found.append(other)
        return found

    def spot(p):
        q = lax.div(p, lay)
        return lax.rem(p + q, lay), pl.multiple_of(q * rows, rows)

    others = mirrors(me, n)
    spots = [spot(p) for p in others]
    home_x, home_y = spot(me)
    own_q = lax.div(me, lay)
    turns = mirrors(own_q, per) + [own_q]

    barrier = pltpu.get_barrier_semaphore()

    for p in others:
        pl.semaphore_signal(barrier, inc=1, device_id={"inst": p}, device_id_type=MESH)

    @pl.when(has_lo)
    def _():
        pl.semaphore_signal(barrier, inc=1, device_id={"cells": cell - 1}, device_id_type=MESH)

    @pl.when(has_hi)
    def _():
        pl.semaphore_signal(barrier, inc=1, device_id={"cells": cell + 1}, device_id_type=MESH)

    local = [
        (adj, vp.at[0, :, 2 : 2 + lay, mid, :]),
        (dt, uh.at[0, nv]),
        (c2.at[0], cx.at[0, 2 : 2 + lay]),
        (c4.at[0], cx.at[1, 2 : 2 + lay]),
        (c2.at[1], cy.at[0, :, mid, :]),
        (c4.at[1], cy.at[1, :, mid, :]),
        (c2.at[2], cz.at[0]),
        (c4.at[2], cz.at[1]),
        (grad, gv),
        (jac, jv),
        (freq_in, freq),
        (damp_in, damp),
    ]
    local = [pltpu.make_async_copy(s, d, loc_sem.at[i]) for i, (s, d) in enumerate(local)]
    for c in local:
        c.start()
    dtv = uh.at[0, nv]

    def wait_bytes(ref, sem):
        pltpu.make_async_copy(ref, ref, sem).wait()

    def width(unit):
        return nv + 1 if unit == 1 else nv

    def owner_rows(p):
        return pl.ds(pl.multiple_of(p * rows, rows), rows)

    def chunk_at(unit, x, y):
        if unit == 0:
            return vp.at[0, :, 2 + x, pl.ds(pl.multiple_of(PAD + y, rows), rows), :]
        return uh.at[unit - 1, 0 : width(unit), x, pl.ds(y, rows), :]

    def send_out(unit, p, x, y):
        pltpu.make_async_remote_copy(
            src_ref=chunk_at(unit, x, y), dst_ref=tb.at[unit, 0 : width(unit), owner_rows(me), :],
            send_sem=ss.at[unit], recv_sem=trs.at[unit],
            device_id={"inst": p}, device_id_type=MESH,
        ).start()

    def keep_out(unit):
        pltpu.make_async_copy(
            chunk_at(unit, home_x, home_y), tb.at[unit, 0 : width(unit), owner_rows(me), :],
            trs.at[unit],
        ).start()

    def send_home(s):
        dst = mh.at[s, :, home_x, pl.ds(home_y, rows), :]
        for p in others:
            pltpu.make_async_remote_copy(
                src_ref=mt.at[s, :, owner_rows(p), :], dst_ref=dst,
                send_sem=ss.at[SECTIONS + s], recv_sem=mrs.at[s, home_x],
                device_id={"inst": p}, device_id_type=MESH,
            ).start()
        pltpu.make_async_copy(mt.at[s, :, owner_rows(me), :], dst, mrs.at[s, home_x]).start()

    def halo_up(s):
        return pltpu.make_async_remote_copy(
            src_ref=vp.at[s, :, lay : lay + 2, mid, :], dst_ref=hb.at[s, 0],
            send_sem=hss.at[s, 0], recv_sem=hrs.at[s, 0],
            device_id={"cells": cell + 1}, device_id_type=MESH,
        )

    def halo_down(s):
        return pltpu.make_async_remote_copy(
            src_ref=vp.at[s, :, 2:4, mid, :], dst_ref=hb.at[s, 1],
            send_sem=hss.at[s, 1], recv_sem=hrs.at[s, 1],
            device_id={"cells": cell - 1}, device_id_type=MESH,
        )

    coef_up = pltpu.make_async_remote_copy(
        src_ref=cx.at[:, lay : lay + 2], dst_ref=cx.at[:, 0:2],
        send_sem=chs.at[0], recv_sem=chr_.at[0],
        device_id={"cells": cell + 1}, device_id_type=MESH,
    )
    coef_down = pltpu.make_async_remote_copy(
        src_ref=cx.at[:, 2:4], dst_ref=cx.at[:, 2 + lay : 4 + lay],
        send_sem=chs.at[1], recv_sem=chr_.at[1],
        device_id={"cells": cell - 1}, device_id_type=MESH,
    )

    def start_pair(up, down):
        @pl.when(has_hi)
        def _():
            up.start()

        @pl.when(has_lo)
        def _():
            down.start()

    def land_pair(up, down):
        @pl.when(has_lo)
        def _():
            up.wait_recv()

        @pl.when(has_hi)
        def _():
            down.wait_recv()

    def sent_pair(up, down):
        @pl.when(has_hi)
        def _():
            up.wait_send()

        @pl.when(has_lo)
        def _():
            down.wait_send()

    lanes = lax.broadcasted_iota(jnp.int32, (ny, nz), 1)
    keep_lo = jnp.where(lanes >= 1, 1.0, 0.0)
    keep_hi = jnp.where(lanes < nz - 1, 1.0, 0.0)

    def stencil_plane():
        @pl.loop(0, lay)
        def _(x):
            up4 = cy[1, x, PAD + 1 : PAD + 1 + ny, :]
            here3 = 3.0 * cy[1, x, mid, :] + cy[0, x, mid, :]
            low = slice(PAD - 1, PAD - 1 + ny)
            below3 = 3.0 * cy[1, x, low, :] + cy[0, x, low, :]
            below4 = cy[1, x, PAD - 2 : PAD - 2 + ny, :]
            kk[4, x] = below4
            kk[5, x] = -(below3 + below4)
            kk[6, x] = -(up4 + here3)
            kk[7, x] = up4
            centre = here3 + below3
            here4 = cz[1, x]
            here3 = 3.0 * here4 + cz[0, x]
            up4 = jnp.where(lanes < nz - 1, pltpu.roll(here4, nz - 1, 1), 0.0)
            below3 = jnp.where(lanes >= 1, pltpu.roll(here3, 1, 1), 0.0)
            below4 = jnp.where(lanes >= 2, pltpu.roll(here4, 2, 1), 0.0)
            kk[8, x] = below4
            kk[9, x] = jnp.where(lanes >= 1, -(below3 + below4), 0.0)
            kk[10, x] = jnp.where(lanes < nz - 1, -(up4 + here3), 0.0)
            kk[11, x] = jnp.where(lanes < nz - 2, up4, 0.0)
            kk[12, x] = centre + here3 + below3

    def stencil_layers():
        @pl.loop(0, lay)
        def _(x):
            up4 = cx[1, x + 3]
            here3 = 3.0 * cx[1, x + 2] + cx[0, x + 2]
            below3 = 3.0 * cx[1, x + 1] + cx[0, x + 1]
            below4 = cx[1, x]
            kk[0, x] = below4
            kk[1, x] = -(below3 + below4)
            kk[2, x] = -(up4 + here3)
            kk[3, x] = up4
            kk[12, x] += here3 + below3

    def send_layer(s, x):
        for i, q in enumerate(turns):
            p = q * lay + lax.rem(x + (lay * per - q), lay)
            y = pl.multiple_of(q * rows, rows)
            if i < per - 1:
                send_out(s + 1, p, x, y)
            else:
                @pl.when(x != home_x)
                def _():
                    send_out(s + 1, p, x, y)

                @pl.when(x == home_x)
                def _():
                    keep_out(s + 1)

    def spatial(s, sending):
        factor = FACTORS[s]
        first, last = 2 * lo, lay - 2 * hi

        @pl.loop(0, lay)
        def _(i):
            x = back * (lay - 1 - i) + (1 - back) * i
            sums, central = [], [[], [], []]
            for b in range(nv):
                v0 = vp[s, b, x + 2, mid, :]
                total = kk[12, x] * v0 + gv[b, x]
                m2, m1 = vp[s, b, x, mid, :], vp[s, b, x + 1, mid, :]
                p1, p2 = vp[s, b, x + 3, mid, :], vp[s, b, x + 4, mid, :]
                total += kk[0, x] * m2 + kk[1, x] * m1 + kk[2, x] * p1 + kk[3, x] * p2
                central[0].append(m1 - p1)
                m2, m1, p1, p2 = (
                    vp[s, b, x + 2, PAD + o : PAD + o + ny, :] for o in (-2, -1, 1, 2)
                )
                total += kk[4, x] * m2 + kk[5, x] * m1 + kk[6, x] * p1 + kk[7, x] * p2
                central[1].append(m1 - p1)
                m2, m1, p1, p2 = (pltpu.roll(v0, o, 1) for o in (2, 1, nz - 1, nz - 2))
                total += kk[8, x] * m2 + kk[9, x] * m1 + kk[10, x] * p1 + kk[11, x] * p2
                central[2].append(keep_lo * m1 - keep_hi * p1)
                sums.append(total)
            step = factor * dtv[x]
            for b in range(nv):
                flux = jv[0, 0, b, x] * central[0][0]
                for d in range(3):
                    for a in range(nv):
                        if d or a:
                            flux += jv[d, a, b, x] * central[d][a]
                uh[s, b, x] = vp[0, b, x + 2, mid, :] - step * (sums[b] + 0.5 * flux)

            if sending:
                @pl.when(jnp.logical_and(x >= first, x < last))
                def _():
                    send_layer(s, x)

        def edge(x, side, near, far, k_near, k_far, sign):
            step = factor * dtv[x]
            for b in range(nv):
                flux = jv[0, 0, b, x] * hb[s, side, 0, near]
                for a in range(1, nv):
                    flux += jv[0, a, b, x] * hb[s, side, a, near]
                total = kk[k_near, x] * hb[s, side, b, near] + kk[k_far, x] * hb[s, side, b, far]
                uh[s, b, x] -= step * (total + sign * flux)

        def rim(x, side, near, k_far):
            step = factor * dtv[x]
            for b in range(nv):
                uh[s, b, x] -= step * (kk[k_far, x] * hb[s, side, b, near])

        @pl.when(has_lo)
        def _():
            halo_up(s).wait_recv()
            edge(0, 0, 1, 0, 1, 0, 0.5)
            rim(1, 0, 1, 0)

        @pl.when(has_hi)
        def _():
            halo_down(s).wait_recv()
            edge(lay - 1, 1, 0, 1, 2, 3, -0.5)
            rim(lay - 2, 1, 0, 3)

        if sending:
            @pl.loop(0, lay)
            def _(x):
                @pl.when(jnp.logical_or(x < first, x >= last))
                def _():
                    send_layer(s, x)

    def home_step(s):
        factor = FACTORS[s - 1]
        ready = 2 * (1 - both) + lay * both

        @pl.loop(0, lay)
        def _(i):
            x = back * i + (1 - back) * (lay - 1 - i)
            wait_bytes(mh.at[s - 1, :, x], mrs.at[s - 1, x])
            step = factor * dtv[x]
            for b in range(nv):
                vp[s, b, 2 + x, mid, :] = uh[s - 1, b, x] - step * mh[s - 1, b, x]

            @pl.when(i == ready - 1)
            def _():
                start_pair(halo_up(s), halo_down(s))

    def mix(s, value):
        @pl.loop(0, nv)
        def _(b):
            weights = [kv[i] for i in range(n)]
            turned = []
            for j in range(groups):
                v = value(b, slice(j * TILE, (j + 1) * TILE))
                turned.append([v] + [pltpu.roll(v, TILE - r * rows, 0) for r in range(1, pack)])
            for k in range(groups):
                total = None
                for j in range(groups):
                    for r in range(pack):
                        term = weights[(j - k) % groups * pack + r] * turned[j][r]
                        total = term if total is None else total + term
                mt[s, b, k * TILE : (k + 1) * TILE, :] = total

        send_home(s)

    def owner_start():
        wait_bytes(tb.at[0, 0:nv], trs.at[0])
        mix(0, lambda b, r: tb[0, b, r, :])

    def owner_step(s):
        wait_bytes(tb.at[s, 0 : width(s)], trs.at[s])
        factor = FACTORS[s - 1]
        mix(s, lambda b, r: tb[s, b, r, :] - factor * (tb[1, nv, r, :] * mt[s - 1, b, r, :]))

    def send_all(s):
        @pl.loop(0, lay)
        def _(x):
            send_layer(s, x)

    slope, curve = coupling_tables(n)
    part = lax.broadcasted_iota(jnp.int32, (TILE, nz), 0) // rows
    local[10].wait()
    local[11].wait()
    for j in range(groups):
        for r in range(pack):
            rise = jnp.zeros((TILE, nz), jnp.float32)
            bend = jnp.zeros((TILE, nz), jnp.float32)
            for h in range(pack):
                m = (j * pack + (h + r) % pack - h) % n
                rise = jnp.where(part == h, slope[m], rise)
                bend = jnp.where(part == h, curve[m], bend)
            kv[j * pack + r] = freq[0] * rise + damp[0] * bend
    for s in range(SECTIONS):
        vp[s, :, 2 : 2 + lay, 0:PAD, :] = jnp.zeros((nv, lay, PAD, nz), jnp.float32)
        vp[s, :, 2 : 2 + lay, PAD + ny :, :] = jnp.zeros((nv, lay, PAD, nz), jnp.float32)
        vp[s, :, 0:2, mid, :] = jnp.zeros((nv, 2, ny, nz), jnp.float32)
        vp[s, :, 2 + lay :, mid, :] = jnp.zeros((nv, 2, ny, nz), jnp.float32)
    cy[:, :, 0:PAD, :] = jnp.zeros((2, lay, PAD, nz), jnp.float32)
    cy[:, :, PAD + ny :, :] = jnp.zeros((2, lay, PAD, nz), jnp.float32)

    @pl.when(jnp.logical_not(has_lo))
    def _():
        cx[:, 0:2] = jnp.zeros((2, 2, ny, nz), jnp.float32)

    @pl.when(jnp.logical_not(has_hi))
    def _():
        cx[:, 2 + lay :] = jnp.zeros((2, 2, ny, nz), jnp.float32)

    local[0].wait()
    local[2].wait()
    local[3].wait()
    pl.semaphore_wait(barrier, n - 1 + lo + hi)

    for p, (x, y) in zip(others, spots):
        send_out(0, p, x, y)
    keep_out(0)
    start_pair(coef_up, coef_down)
    start_pair(halo_up(0), halo_down(0))
    for c in [local[1]] + local[4:10]:
        c.wait()
    stencil_plane()
    land_pair(coef_up, coef_down)
    stencil_layers()
    spatial(0, False)
    owner_start()
    send_all(0)
    home_step(1)
    spatial(1, True)
    owner_step(1)
    owner_step(2)
    home_step(2)
    spatial(2, True)
    home_step(3)
    spatial(3, True)
    owner_step(3)
    owner_step(4)
    home_step(4)
    spatial(4, False)

    @pl.loop(0, lay)
    def _(x):
        wait_bytes(mh.at[4, :, x], mrs.at[4, x])
        step = FACTORS[4] * dtv[x]
        for b in range(nv):
            out[b, x] = uh[4, b, x] - step * mh[4, b, x]

    for unit in range(SECTIONS):
        wait_bytes(tb.at[unit, 0 : width(unit), 0 : (n - 1) * rows, :], ss.at[unit])
        wait_bytes(mt.at[unit, :, 0 : (n - 1) * rows, :], ss.at[SECTIONS + unit])
    for s in range(SECTIONS):
        sent_pair(halo_up(s), halo_down(s))
    sent_pair(coef_up, coef_down)


def on_device(n, cells, adjoint, grad, jac, c2, c4, dt, freq, damp):
    nv, lay, ny, nz = adjoint.shape[1:]
    rows = lay * ny // n
    assert rows * n == lay * ny and ny % rows == 0 and lay >= 2
    assert TILE % rows == 0 and (n * rows) % TILE == 0
    f32 = jnp.float32
    anywhere = pl.BlockSpec(memory_space=pl.ANY)
    dma = pltpu.SemaphoreType.DMA
    tall = ny + 2 * PAD
    result = pl.pallas_call(
        functools.partial(kernel, n, cells),
        out_shape=pltpu.VMEM(adjoint.shape[1:], f32),
        in_specs=[anywhere] * 8,
        out_specs=pl.BlockSpec(memory_space=pltpu.VMEM),
        scratch_shapes=[
            pltpu.VMEM((SECTIONS, nv, lay + 4, tall, nz), f32),
            pltpu.VMEM(jac.shape[1:], f32),
            pltpu.VMEM((2, lay + 4, ny, nz), f32),
            pltpu.VMEM((2, lay, tall, nz), f32),
            pltpu.VMEM((2, lay, ny, nz), f32),
            pltpu.VMEM((13, lay, ny, nz), f32),
            pltpu.VMEM((nv, lay, ny, nz), f32),
            pltpu.VMEM((SECTIONS, nv + 1, lay, ny, nz), f32),
            pltpu.VMEM((SECTIONS, nv, lay, ny, nz), f32),
            pltpu.VMEM((SECTIONS, nv + 1, n * rows, nz), f32),
            pltpu.VMEM((SECTIONS, nv, n * rows, nz), f32),
            pltpu.VMEM((SECTIONS, 2, nv, 2, ny, nz), f32),
            pltpu.VMEM((n, TILE, nz), f32),
            pltpu.SMEM((1,), f32),
            pltpu.SMEM((1,), f32),
            dma((12,)),
            dma((2 * SECTIONS,)),
            dma((SECTIONS,)),
            dma((SECTIONS, lay)),
            dma((SECTIONS, 2)),
            dma((SECTIONS, 2)),
            dma((2,)),
            dma((2,)),
        ],
        compiler_params=pltpu.CompilerParams(collective_id=0, has_side_effects=True),
    )(adjoint[0], grad[0], jac[0], c2[0], c4[0], dt[0], freq, damp)
    return result[None]


def solution(mesh):
    placed = (
        P("inst", None, "cells", None, None),
        P("inst", None, "cells", None, None),
        P("inst", None, None, None, "cells", None, None),
        P("inst", None, "cells", None, None),
        P("inst", None, "cells", None, None),
        P("inst", "cells", None, None),
        P(),
        P(),
    )
    return jax.shard_map(
        functools.partial(on_device, mesh.shape["inst"], mesh.shape["cells"]),
        mesh=mesh,
        in_specs=placed,
        out_specs=P("inst", None, "cells", None, None),
        check_vma=False,
    )
```

```python
import functools
import math

import jax
import jax.numpy as jnp
from jax import lax
from jax.experimental import pallas as pl
from jax.experimental.pallas import tpu as pltpu
from jax.sharding import PartitionSpec as P

FACTORS = (0.25, 1.0 / 6.0, 0.375, 0.5, 1.0)
SECTIONS = len(FACTORS)
PAD = 8
TILE = 8
MESH = pl.DeviceIdType.MESH


def coupling_tables(count):
    slope, curve = [0.0], [count * count / 12.0 + 1.0 / 6.0]
    for m in range(1, count):
        parity = 1.0 if m % 2 == 0 else -1.0
        angle = math.pi * m / count
        slope.append(0.5 * parity * math.cos(angle) / math.sin(angle))
        curve.append(0.5 * parity / math.sin(angle) ** 2)
    return slope, curve


def kernel(
    n, cells, adj, grad, jac, c2, c4, dt, freq_in, damp_in, out,
    vp, jv, cx, cy, cz, kk, gv, uh, mh, tb, mt, hb, kv, freq, damp,
    loc_sem, ss, trs, mrs, hss, hrs, chs, chr_,
):
    nv, lay, ny, nz = adj.shape
    rows = lay * ny // n
    per = ny // rows
    pack = TILE // rows
    groups = n // pack
    me = lax.axis_index("inst")
    cell = lax.axis_index("cells")
    has_lo = cell > 0
    has_hi = cell < cells - 1
    lo = has_lo.astype(jnp.int32)
    hi = has_hi.astype(jnp.int32)
    both = lo * hi
    back = lo * (1 - both)
    mid = slice(PAD, PAD + ny)

    def mirrors(value, count):
        if count & (count - 1):
            return [lax.rem(value + i, count) for i in range(1, count)]
        moves, bit = [], 1
        while bit < count:
            moves.append((bit, bit - 2 * bit * lax.rem(lax.div(value, bit), 2)))
            bit *= 2
        found = []
        for flip in range(count - 1, 0, -1):
            other = value
            for bit, move in moves:
                if flip & bit:
                    other = other + move
            found.append(other)
        return found

    def spot(p):
        q = lax.div(p, lay)
        return lax.rem(p + q, lay), pl.multiple_of(q * rows, rows)

    others = mirrors(me, n)
    spots = [spot(p) for p in others]
    home_x, home_y = spot(me)
    own_q = lax.div(me, lay)
    turns = mirrors(own_q, per) + [own_q]

    barrier = pltpu.get_barrier_semaphore()

    for p in others:
        pl.semaphore_signal(barrier, inc=1, device_id={"inst": p}, device_id_type=MESH)

    @pl.when(has_lo)
    def _():
        pl.semaphore_signal(barrier, inc=1, device_id={"cells": cell - 1}, device_id_type=MESH)

    @pl.when(has_hi)
    def _():
        pl.semaphore_signal(barrier, inc=1, device_id={"cells": cell + 1}, device_id_type=MESH)

    local = [
        (adj, vp.at[0, :, 2 : 2 + lay, mid, :]),
        (dt, uh.at[0, nv]),
        (c2.at[0], cx.at[0, 2 : 2 + lay]),
        (c4.at[0], cx.at[1, 2 : 2 + lay]),
        (c2.at[1], cy.at[0, :, mid, :]),
        (c4.at[1], cy.at[1, :, mid, :]),
        (c2.at[2], cz.at[0]),
        (c4.at[2], cz.at[1]),
        (grad, gv),
        (jac, jv),
        (freq_in, freq),
        (damp_in, damp),
    ]
    local = [pltpu.make_async_copy(s, d, loc_sem.at[i]) for i, (s, d) in enumerate(local)]
    for c in local:
        c.start()
    dtv = uh.at[0, nv]

    def wait_bytes(ref, sem):
        pltpu.make_async_copy(ref, ref, sem).wait()

    def owner_rows(p):
        return pl.ds(pl.multiple_of(p * rows, rows), rows)

    def chunk_at(unit, x, y):
        if unit == 0:
            return vp.at[0, :, 2 + x, pl.ds(pl.multiple_of(PAD + y, rows), rows), :]
        return uh.at[unit - 1, 0:nv, x, pl.ds(y, rows), :]

    def send_out(unit, p, x, y):
        pltpu.make_async_remote_copy(
            src_ref=chunk_at(unit, x, y), dst_ref=tb.at[unit, 0:nv, owner_rows(me), :],
            send_sem=ss.at[unit], recv_sem=trs.at[unit],
            device_id={"inst": p}, device_id_type=MESH,
        ).start()

    def keep_out(unit):
        pltpu.make_async_copy(
            chunk_at(unit, home_x, home_y), tb.at[unit, 0:nv, owner_rows(me), :],
            trs.at[unit],
        ).start()

    def send_steps():
        dst = tb.at[1, nv, owner_rows(me), :]
        for p, (x, y) in zip(others, spots):
            pltpu.make_async_remote_copy(
                src_ref=uh.at[0, nv, x, pl.ds(y, rows), :], dst_ref=dst,
                send_sem=ss.at[2 * SECTIONS], recv_sem=trs.at[SECTIONS],
                device_id={"inst": p}, device_id_type=MESH,
            ).start()
        pltpu.make_async_copy(
            uh.at[0, nv, home_x, pl.ds(home_y, rows), :], dst, trs.at[SECTIONS]
        ).start()

    def send_home(s):
        dst = mh.at[s, :, home_x, pl.ds(home_y, rows), :]
        for p in others:
            pltpu.make_async_remote_copy(
                src_ref=mt.at[s, :, owner_rows(p), :], dst_ref=dst,
                send_sem=ss.at[SECTIONS + s], recv_sem=mrs.at[s, home_x],
                device_id={"inst": p}, device_id_type=MESH,
            ).start()
        pltpu.make_async_copy(mt.at[s, :, owner_rows(me), :], dst, mrs.at[s, home_x]).start()

    def halo_up(s):
        return pltpu.make_async_remote_copy(
            src_ref=vp.at[s, :, lay : lay + 2, mid, :], dst_ref=hb.at[s, 0],
            send_sem=hss.at[s, 0], recv_sem=hrs.at[s, 0],
            device_id={"cells": cell + 1}, device_id_type=MESH,
        )

    def halo_down(s):
        return pltpu.make_async_remote_copy(
            src_ref=vp.at[s, :, 2:4, mid, :], dst_ref=hb.at[s, 1],
            send_sem=hss.at[s, 1], recv_sem=hrs.at[s, 1],
            device_id={"cells": cell - 1}, device_id_type=MESH,
        )

    coef_up = pltpu.make_async_remote_copy(
        src_ref=cx.at[:, lay : lay + 2], dst_ref=cx.at[:, 0:2],
        send_sem=chs.at[0], recv_sem=chr_.at[0],
        device_id={"cells": cell + 1}, device_id_type=MESH,
    )
    coef_down = pltpu.make_async_remote_copy(
        src_ref=cx.at[:, 2:4], dst_ref=cx.at[:, 2 + lay : 4 + lay],
        send_sem=chs.at[1], recv_sem=chr_.at[1],
        device_id={"cells": cell - 1}, device_id_type=MESH,
    )

    def start_pair(up, down):
        @pl.when(has_hi)
        def _():
            up.start()

        @pl.when(has_lo)
        def _():
            down.start()

    def land_pair(up, down):
        @pl.when(has_lo)
        def _():
            up.wait_recv()

        @pl.when(has_hi)
        def _():
            down.wait_recv()

    def sent_pair(up, down):
        @pl.when(has_hi)
        def _():
            up.wait_send()

        @pl.when(has_lo)
        def _():
            down.wait_send()

    lanes = lax.broadcasted_iota(jnp.int32, (ny, nz), 1)
    keep_lo = jnp.where(lanes >= 1, 1.0, 0.0)
    keep_hi = jnp.where(lanes < nz - 1, 1.0, 0.0)

    def stencil_plane():
        @pl.loop(0, lay)
        def _(x):
            up4 = cy[1, x, PAD + 1 : PAD + 1 + ny, :]
            here3 = 3.0 * cy[1, x, mid, :] + cy[0, x, mid, :]
            low = slice(PAD - 1, PAD - 1 + ny)
            below3 = 3.0 * cy[1, x, low, :] + cy[0, x, low, :]
            below4 = cy[1, x, PAD - 2 : PAD - 2 + ny, :]
            kk[4, x] = below4
            kk[5, x] = -(below3 + below4)
            kk[6, x] = -(up4 + here3)
            kk[7, x] = up4
            centre = here3 + below3
            here4 = cz[1, x]
            here3 = 3.0 * here4 + cz[0, x]
            up4 = jnp.where(lanes < nz - 1, pltpu.roll(here4, nz - 1, 1), 0.0)
            below3 = jnp.where(lanes >= 1, pltpu.roll(here3, 1, 1), 0.0)
            below4 = jnp.where(lanes >= 2, pltpu.roll(here4, 2, 1), 0.0)
            kk[8, x] = below4
            kk[9, x] = jnp.where(lanes >= 1, -(below3 + below4), 0.0)
            kk[10, x] = jnp.where(lanes < nz - 1, -(up4 + here3), 0.0)
            kk[11, x] = jnp.where(lanes < nz - 2, up4, 0.0)
            kk[12, x] = centre + here3 + below3

    def stencil_layers():
        @pl.loop(0, lay)
        def _(x):
            up4 = cx[1, x + 3]
            here3 = 3.0 * cx[1, x + 2] + cx[0, x + 2]
            below3 = 3.0 * cx[1, x + 1] + cx[0, x + 1]
            below4 = cx[1, x]
            kk[0, x] = below4
            kk[1, x] = -(below3 + below4)
            kk[2, x] = -(up4 + here3)
            kk[3, x] = up4
            kk[12, x] += here3 + below3

    def send_layer(s, x):
        for i, q in enumerate(turns):
            p = q * lay + lax.rem(x + (lay * per - q), lay)
            y = pl.multiple_of(q * rows, rows)
            if i < per - 1:
                send_out(s + 1, p, x, y)
            else:
                @pl.when(x != home_x)
                def _():
                    send_out(s + 1, p, x, y)

                @pl.when(x == home_x)
                def _():
                    keep_out(s + 1)

    def spatial(s, sending):
        factor = FACTORS[s]
        first, last = 2 * lo, lay - 2 * hi

        @pl.loop(0, lay)
        def _(i):
            x = back * (lay - 1 - i) + (1 - back) * i
            sums, central = [], [[], [], []]
            for b in range(nv):
                v0 = vp[s, b, x + 2, mid, :]
                total = kk[12, x] * v0 + gv[b, x]
                m2, m1 = vp[s, b, x, mid, :], vp[s, b, x + 1, mid, :]
                p1, p2 = vp[s, b, x + 3, mid, :], vp[s, b, x + 4, mid, :]
                total += kk[0, x] * m2 + kk[1, x] * m1 + kk[2, x] * p1 + kk[3, x] * p2
                central[0].append(m1 - p1)
                m2, m1, p1, p2 = (
                    vp[s, b, x + 2, PAD + o : PAD + o + ny, :] for o in (-2, -1, 1, 2)
                )
                total += kk[4, x] * m2 + kk[5, x] * m1 + kk[6, x] * p1 + kk[7, x] * p2
                central[1].append(m1 - p1)
                m2, m1, p1, p2 = (pltpu.roll(v0, o, 1) for o in (2, 1, nz - 1, nz - 2))
                total += kk[8, x] * m2 + kk[9, x] * m1 + kk[10, x] * p1 + kk[11, x] * p2
                central[2].append(keep_lo * m1 - keep_hi * p1)
                sums.append(total)
            step = factor * dtv[x]
            for b in range(nv):
                flux = jv[0, 0, b, x] * central[0][0]
                for d in range(3):
                    for a in range(nv):
                        if d or a:
                            flux += jv[d, a, b, x] * central[d][a]
                uh[s, b, x] = vp[0, b, x + 2, mid, :] - step * (sums[b] + 0.5 * flux)

            if sending:
                @pl.when(jnp.logical_and(x >= first, x < last))
                def _():
                    send_layer(s, x)

        def edge(x, side, near, far, k_near, k_far, sign):
            step = factor * dtv[x]
            for b in range(nv):
                flux = jv[0, 0, b, x] * hb[s, side, 0, near]
                for a in range(1, nv):
                    flux += jv[0, a, b, x] * hb[s, side, a, near]
                total = kk[k_near, x] * hb[s, side, b, near] + kk[k_far, x] * hb[s, side, b, far]
                uh[s, b, x] -= step * (total + sign * flux)

        def rim(x, side, near, k_far):
            step = factor * dtv[x]
            for b in range(nv):
                uh[s, b, x] -= step * (kk[k_far, x] * hb[s, side, b, near])

        @pl.when(has_lo)
        def _():
            halo_up(s).wait_recv()
            edge(0, 0, 1, 0, 1, 0, 0.5)
            rim(1, 0, 1, 0)

        @pl.when(has_hi)
        def _():
            halo_down(s).wait_recv()
            edge(lay - 1, 1, 0, 1, 2, 3, -0.5)
            rim(lay - 2, 1, 0, 3)

        if sending:
            @pl.loop(0, lay)
            def _(x):
                @pl.when(jnp.logical_or(x < first, x >= last))
                def _():
                    send_layer(s, x)

    def home_step(s):
        factor = FACTORS[s - 1]
        ready = 2 * (1 - both) + lay * both

        @pl.loop(0, lay)
        def _(i):
            x = back * i + (1 - back) * (lay - 1 - i)
            wait_bytes(mh.at[s - 1, :, x], mrs.at[s - 1, x])
            step = factor * dtv[x]
            for b in range(nv):
                vp[s, b, 2 + x, mid, :] = uh[s - 1, b, x] - step * mh[s - 1, b, x]

            @pl.when(i == ready - 1)
            def _():
                start_pair(halo_up(s), halo_down(s))

    def mix(s, value):
        @pl.loop(0, nv)
        def _(b):
            weights = [kv[i] for i in range(n)]
            turned = []
            for j in range(groups):
                v = value(b, slice(j * TILE, (j + 1) * TILE))
                turned.append([v] + [pltpu.roll(v, TILE - r * rows, 0) for r in range(1, pack)])
            for k in range(groups):
                total = None
                for j in range(groups):
                    for r in range(pack):
                        term = weights[(j - k) % groups * pack + r] * turned[j][r]
                        total = term if total is None else total + term
                mt[s, b, k * TILE : (k + 1) * TILE, :] = total

        send_home(s)

    def owner_start():
        wait_bytes(tb.at[0, 0:nv], trs.at[0])
        mix(0, lambda b, r: tb[0, b, r, :])

    def owner_step(s):
        wait_bytes(tb.at[s, 0:nv], trs.at[s])
        if s == 1:
            wait_bytes(tb.at[1, nv], trs.at[SECTIONS])
        factor = FACTORS[s - 1]
        mix(s, lambda b, r: tb[s, b, r, :] - factor * (tb[1, nv, r, :] * mt[s - 1, b, r, :]))

    def send_all(s):
        @pl.loop(0, lay)
        def _(x):
            send_layer(s, x)

    slope, curve = coupling_tables(n)
    part = lax.broadcasted_iota(jnp.int32, (TILE, nz), 0) // rows
    local[10].wait()
    local[11].wait()
    for j in range(groups):
        for r in range(pack):
            rise = jnp.zeros((TILE, nz), jnp.float32)
            bend = jnp.zeros((TILE, nz), jnp.float32)
            for h in range(pack):
                m = (j * pack + (h + r) % pack - h) % n
                rise = jnp.where(part == h, slope[m], rise)
                bend = jnp.where(part == h, curve[m], bend)
            kv[j * pack + r] = freq[0] * rise + damp[0] * bend
    for s in range(SECTIONS):
        vp[s, :, 2 : 2 + lay, 0:PAD, :] = jnp.zeros((nv, lay, PAD, nz), jnp.float32)
        vp[s, :, 2 : 2 + lay, PAD + ny :, :] = jnp.zeros((nv, lay, PAD, nz), jnp.float32)
        vp[s, :, 0:2, mid, :] = jnp.zeros((nv, 2, ny, nz), jnp.float32)
        vp[s, :, 2 + lay :, mid, :] = jnp.zeros((nv, 2, ny, nz), jnp.float32)
    cy[:, :, 0:PAD, :] = jnp.zeros((2, lay, PAD, nz), jnp.float32)
    cy[:, :, PAD + ny :, :] = jnp.zeros((2, lay, PAD, nz), jnp.float32)

    @pl.when(jnp.logical_not(has_lo))
    def _():
        cx[:, 0:2] = jnp.zeros((2, 2, ny, nz), jnp.float32)

    @pl.when(jnp.logical_not(has_hi))
    def _():
        cx[:, 2 + lay :] = jnp.zeros((2, 2, ny, nz), jnp.float32)

    local[0].wait()
    local[2].wait()
    local[3].wait()
    pl.semaphore_wait(barrier, n - 1 + lo + hi)

    for p, (x, y) in zip(others, spots):
        send_out(0, p, x, y)
    keep_out(0)
    start_pair(coef_up, coef_down)
    start_pair(halo_up(0), halo_down(0))
    local[1].wait()
    send_steps()
    for c in local[4:10]:
        c.wait()
    stencil_plane()
    land_pair(coef_up, coef_down)
    stencil_layers()
    spatial(0, False)
    owner_start()
    send_all(0)
    home_step(1)
    spatial(1, True)
    owner_step(1)
    owner_step(2)
    home_step(2)
    spatial(2, True)
    home_step(3)
    spatial(3, True)
    owner_step(3)
    owner_step(4)
    home_step(4)
    spatial(4, False)

    @pl.loop(0, lay)
    def _(x):
        wait_bytes(mh.at[4, :, x], mrs.at[4, x])
        step = FACTORS[4] * dtv[x]
        for b in range(nv):
            out[b, x] = uh[4, b, x] - step * mh[4, b, x]

    for unit in range(SECTIONS):
        wait_bytes(tb.at[unit, 0:nv, 0 : (n - 1) * rows, :], ss.at[unit])
        wait_bytes(mt.at[unit, :, 0 : (n - 1) * rows, :], ss.at[SECTIONS + unit])
    wait_bytes(tb.at[1, nv, 0 : (n - 1) * rows, :], ss.at[2 * SECTIONS])
    for s in range(SECTIONS):
        sent_pair(halo_up(s), halo_down(s))
    sent_pair(coef_up, coef_down)


def on_device(n, cells, adjoint, grad, jac, c2, c4, dt, freq, damp):
    nv, lay, ny, nz = adjoint.shape[1:]
    rows = lay * ny // n
    assert rows * n == lay * ny and ny % rows == 0 and lay >= 2
    assert TILE % rows == 0 and (n * rows) % TILE == 0
    f32 = jnp.float32
    anywhere = pl.BlockSpec(memory_space=pl.ANY)
    dma = pltpu.SemaphoreType.DMA
    tall = ny + 2 * PAD
    result = pl.pallas_call(
        functools.partial(kernel, n, cells),
        out_shape=pltpu.VMEM(adjoint.shape[1:], f32),
        in_specs=[anywhere] * 8,
        out_specs=pl.BlockSpec(memory_space=pltpu.VMEM),
        scratch_shapes=[
            pltpu.VMEM((SECTIONS, nv, lay + 4, tall, nz), f32),
            pltpu.VMEM(jac.shape[1:], f32),
            pltpu.VMEM((2, lay + 4, ny, nz), f32),
            pltpu.VMEM((2, lay, tall, nz), f32),
            pltpu.VMEM((2, lay, ny, nz), f32),
            pltpu.VMEM((13, lay, ny, nz), f32),
            pltpu.VMEM((nv, lay, ny, nz), f32),
            pltpu.VMEM((SECTIONS, nv + 1, lay, ny, nz), f32),
            pltpu.VMEM((SECTIONS, nv, lay, ny, nz), f32),
            pltpu.VMEM((SECTIONS, nv + 1, n * rows, nz), f32),
            pltpu.VMEM((SECTIONS, nv, n * rows, nz), f32),
            pltpu.VMEM((SECTIONS, 2, nv, 2, ny, nz), f32),
            pltpu.VMEM((n, TILE, nz), f32),
            pltpu.SMEM((1,), f32),
            pltpu.SMEM((1,), f32),
            dma((12,)),
            dma((2 * SECTIONS + 1,)),
            dma((SECTIONS + 1,)),
            dma((SECTIONS, lay)),
            dma((SECTIONS, 2)),
            dma((SECTIONS, 2)),
            dma((2,)),
            dma((2,)),
        ],
        compiler_params=pltpu.CompilerParams(collective_id=0, has_side_effects=True),
    )(adjoint[0], grad[0], jac[0], c2[0], c4[0], dt[0], freq, damp)
    return result[None]


def solution(mesh):
    placed = (
        P("inst", None, "cells", None, None),
        P("inst", None, "cells", None, None),
        P("inst", None, None, None, "cells", None, None),
        P("inst", None, "cells", None, None),
        P("inst", None, "cells", None, None),
        P("inst", "cells", None, None),
        P(),
        P(),
    )
    return jax.shard_map(
        functools.partial(on_device, mesh.shape["inst"], mesh.shape["cells"]),
        mesh=mesh,
        in_specs=placed,
        out_specs=P("inst", None, "cells", None, None),
        check_vma=False,
    )
```

```python
import functools
import math

import jax
import jax.numpy as jnp
from jax import lax
from jax.experimental import pallas as pl
from jax.experimental.pallas import tpu as pltpu
from jax.sharding import PartitionSpec as P

FACTORS = (0.25, 1.0 / 6.0, 0.375, 0.5, 1.0)
SECTIONS = len(FACTORS)
PAD = 8
TILE = 8
MESH = pl.DeviceIdType.MESH


def coupling_tables(count):
    slope, curve = [0.0], [count * count / 12.0 + 1.0 / 6.0]
    for m in range(1, count):
        parity = 1.0 if m % 2 == 0 else -1.0
        angle = math.pi * m / count
        slope.append(0.5 * parity * math.cos(angle) / math.sin(angle))
        curve.append(0.5 * parity / math.sin(angle) ** 2)
    return slope, curve


def kernel(
    n, cells, adj, grad, jac, c2, c4, dt, freq_in, damp_in, out,
    vp, jv, cx, cy, cz, kk, gv, uh, mh, tb, mt, hb, kv, freq, damp,
    loc_sem, ss, trs, mrs, hss, hrs, chs, chr_,
):
    nv, lay, ny, nz = adj.shape
    rows = lay * ny // n
    per = ny // rows
    pack = TILE // rows
    groups = n // pack
    me = lax.axis_index("inst")
    cell = lax.axis_index("cells")
    has_lo = cell > 0
    has_hi = cell < cells - 1
    lo = has_lo.astype(jnp.int32)
    hi = has_hi.astype(jnp.int32)
    both = lo * hi
    back = lo * (1 - both)
    mid = slice(PAD, PAD + ny)

    def mirrors(value, count):
        if count & (count - 1):
            return [lax.rem(value + i, count) for i in range(1, count)]
        moves, bit = [], 1
        while bit < count:
            moves.append((bit, bit - 2 * bit * lax.rem(lax.div(value, bit), 2)))
            bit *= 2
        found = []
        for flip in range(count - 1, 0, -1):
            other = value
            for bit, move in moves:
                if flip & bit:
                    other = other + move
            found.append(other)
        return found

    def spot(p):
        q = lax.div(p, lay)
        return lax.rem(p + q, lay), pl.multiple_of(q * rows, rows)

    others = mirrors(me, n)
    spots = [spot(p) for p in others]
    home_x, home_y = spot(me)
    own_q = lax.div(me, lay)
    turns = mirrors(own_q, per) + [own_q]

    barrier = pltpu.get_barrier_semaphore()

    for p in others:
        pl.semaphore_signal(barrier, inc=1, device_id={"inst": p}, device_id_type=MESH)

    @pl.when(has_lo)
    def _():
        pl.semaphore_signal(barrier, inc=1, device_id={"cells": cell - 1}, device_id_type=MESH)

    @pl.when(has_hi)
    def _():
        pl.semaphore_signal(barrier, inc=1, device_id={"cells": cell + 1}, device_id_type=MESH)

    local = [
        (adj, vp.at[0, :, 2 : 2 + lay, mid, :]),
        (dt, uh.at[0, nv]),
        (c2.at[0], cx.at[0, 2 : 2 + lay]),
        (c4.at[0], cx.at[1, 2 : 2 + lay]),
        (c2.at[1], cy.at[0, :, mid, :]),
        (c4.at[1], cy.at[1, :, mid, :]),
        (c2.at[2], cz.at[0]),
        (c4.at[2], cz.at[1]),
        (grad, gv),
        (jac, jv),
        (freq_in, freq),
        (damp_in, damp),
    ]
    local = [pltpu.make_async_copy(s, d, loc_sem.at[i]) for i, (s, d) in enumerate(local)]
    for c in local:
        c.start()
    dtv = uh.at[0, nv]

    def wait_bytes(ref, sem):
        pltpu.make_async_copy(ref, ref, sem).wait()

    def owner_rows(p):
        return pl.ds(pl.multiple_of(p * rows, rows), rows)

    def chunk_at(unit, x, y):
        if unit == 0:
            return vp.at[0, :, 2 + x, pl.ds(pl.multiple_of(PAD + y, rows), rows), :]
        return uh.at[unit - 1, 0:nv, x, pl.ds(y, rows), :]

    def send_out(unit, p, x, y):
        pltpu.make_async_remote_copy(
            src_ref=chunk_at(unit, x, y), dst_ref=tb.at[unit, 0:nv, owner_rows(me), :],
            send_sem=ss.at[unit], recv_sem=trs.at[unit],
            device_id={"inst": p}, device_id_type=MESH,
        ).start()

    def keep_out(unit):
        pltpu.make_async_copy(
            chunk_at(unit, home_x, home_y), tb.at[unit, 0:nv, owner_rows(me), :],
            trs.at[unit],
        ).start()

    def send_steps():
        dst = tb.at[1, nv, owner_rows(me), :]
        for p, (x, y) in zip(others, spots):
            pltpu.make_async_remote_copy(
                src_ref=uh.at[0, nv, x, pl.ds(y, rows), :], dst_ref=dst,
                send_sem=ss.at[2 * SECTIONS], recv_sem=trs.at[SECTIONS],
                device_id={"inst": p}, device_id_type=MESH,
            ).start()
        pltpu.make_async_copy(
            uh.at[0, nv, home_x, pl.ds(home_y, rows), :], dst, trs.at[SECTIONS]
        ).start()

    def send_home(s):
        dst = mh.at[s, :, home_x, pl.ds(home_y, rows), :]
        for p in others:
            pltpu.make_async_remote_copy(
                src_ref=mt.at[s, :, owner_rows(p), :], dst_ref=dst,
                send_sem=ss.at[SECTIONS + s], recv_sem=mrs.at[s, home_x],
                device_id={"inst": p}, device_id_type=MESH,
            ).start()
        pltpu.make_async_copy(mt.at[s, :, owner_rows(me), :], dst, mrs.at[s, home_x]).start()

    def halo_up(s):
        return pltpu.make_async_remote_copy(
            src_ref=vp.at[s, :, lay : lay + 2, mid, :], dst_ref=hb.at[s, 0],
            send_sem=hss.at[s, 0], recv_sem=hrs.at[s, 0],
            device_id={"cells": cell + 1}, device_id_type=MESH,
        )

    def halo_down(s):
        return pltpu.make_async_remote_copy(
            src_ref=vp.at[s, :, 2:4, mid, :], dst_ref=hb.at[s, 1],
            send_sem=hss.at[s, 1], recv_sem=hrs.at[s, 1],
            device_id={"cells": cell - 1}, device_id_type=MESH,
        )

    coef_up = pltpu.make_async_remote_copy(
        src_ref=cx.at[:, lay : lay + 2], dst_ref=cx.at[:, 0:2],
        send_sem=chs.at[0], recv_sem=chr_.at[0],
        device_id={"cells": cell + 1}, device_id_type=MESH,
    )
    coef_down = pltpu.make_async_remote_copy(
        src_ref=cx.at[:, 2:4], dst_ref=cx.at[:, 2 + lay : 4 + lay],
        send_sem=chs.at[1], recv_sem=chr_.at[1],
        device_id={"cells": cell - 1}, device_id_type=MESH,
    )

    def start_pair(up, down):
        @pl.when(has_hi)
        def _():
            up.start()

        @pl.when(has_lo)
        def _():
            down.start()

    def land_pair(up, down):
        @pl.when(has_lo)
        def _():
            up.wait_recv()

        @pl.when(has_hi)
        def _():
            down.wait_recv()

    def sent_pair(up, down):
        @pl.when(has_hi)
        def _():
            up.wait_send()

        @pl.when(has_lo)
        def _():
            down.wait_send()

    lanes = lax.broadcasted_iota(jnp.int32, (ny, nz), 1)
    keep_lo = jnp.where(lanes >= 1, 1.0, 0.0)
    keep_hi = jnp.where(lanes < nz - 1, 1.0, 0.0)

    def stencil_plane():
        @pl.loop(0, lay)
        def _(x):
            up4 = cy[1, x, PAD + 1 : PAD + 1 + ny, :]
            here3 = 3.0 * cy[1, x, mid, :] + cy[0, x, mid, :]
            low = slice(PAD - 1, PAD - 1 + ny)
            below3 = 3.0 * cy[1, x, low, :] + cy[0, x, low, :]
            below4 = cy[1, x, PAD - 2 : PAD - 2 + ny, :]
            kk[4, x] = below4
            kk[5, x] = -(below3 + below4)
            kk[6, x] = -(up4 + here3)
            kk[7, x] = up4
            centre = here3 + below3
            here4 = cz[1, x]
            here3 = 3.0 * here4 + cz[0, x]
            up4 = jnp.where(lanes < nz - 1, pltpu.roll(here4, nz - 1, 1), 0.0)
            below3 = jnp.where(lanes >= 1, pltpu.roll(here3, 1, 1), 0.0)
            below4 = jnp.where(lanes >= 2, pltpu.roll(here4, 2, 1), 0.0)
            kk[8, x] = below4
            kk[9, x] = jnp.where(lanes >= 1, -(below3 + below4), 0.0)
            kk[10, x] = jnp.where(lanes < nz - 1, -(up4 + here3), 0.0)
            kk[11, x] = jnp.where(lanes < nz - 2, up4, 0.0)
            kk[12, x] = centre + here3 + below3

    def stencil_layers():
        @pl.loop(0, lay)
        def _(x):
            up4 = cx[1, x + 3]
            here3 = 3.0 * cx[1, x + 2] + cx[0, x + 2]
            below3 = 3.0 * cx[1, x + 1] + cx[0, x + 1]
            below4 = cx[1, x]
            kk[0, x] = below4
            kk[1, x] = -(below3 + below4)
            kk[2, x] = -(up4 + here3)
            kk[3, x] = up4
            kk[12, x] += here3 + below3

    def send_layer(s, x):
        for i, q in enumerate(turns):
            p = q * lay + lax.rem(x + (lay * per - q), lay)
            y = pl.multiple_of(q * rows, rows)
            if i < per - 1:
                send_out(s + 1, p, x, y)
            else:
                @pl.when(x != home_x)
                def _():
                    send_out(s + 1, p, x, y)

                @pl.when(x == home_x)
                def _():
                    keep_out(s + 1)

    def spatial(s, sending):
        factor = FACTORS[s]
        first, last = 2 * lo, lay - 2 * hi

        @pl.loop(0, lay)
        def _(i):
            x = back * (lay - 1 - i) + (1 - back) * i
            sums, central = [], [[], [], []]
            for b in range(nv):
                v0 = vp[s, b, x + 2, mid, :]
                total = kk[12, x] * v0 + gv[b, x]
                m2, m1 = vp[s, b, x, mid, :], vp[s, b, x + 1, mid, :]
                p1, p2 = vp[s, b, x + 3, mid, :], vp[s, b, x + 4, mid, :]
                total += kk[0, x] * m2 + kk[1, x] * m1 + kk[2, x] * p1 + kk[3, x] * p2
                central[0].append(m1 - p1)
                m2, m1, p1, p2 = (
                    vp[s, b, x + 2, PAD + o : PAD + o + ny, :] for o in (-2, -1, 1, 2)
                )
                total += kk[4, x] * m2 + kk[5, x] * m1 + kk[6, x] * p1 + kk[7, x] * p2
                central[1].append(m1 - p1)
                m2, m1, p1, p2 = (pltpu.roll(v0, o, 1) for o in (2, 1, nz - 1, nz - 2))
                total += kk[8, x] * m2 + kk[9, x] * m1 + kk[10, x] * p1 + kk[11, x] * p2
                central[2].append(keep_lo * m1 - keep_hi * p1)
                sums.append(total)
            step = factor * dtv[x]
            for b in range(nv):
                flux = jv[0, 0, b, x] * central[0][0]
                for d in range(3):
                    for a in range(nv):
                        if d or a:
                            flux += jv[d, a, b, x] * central[d][a]
                uh[s, b, x] = vp[0, b, x + 2, mid, :] - step * (sums[b] + 0.5 * flux)

            if sending:
                @pl.when(jnp.logical_and(x >= first, x < last))
                def _():
                    send_layer(s, x)

        def edge(x, side, near, far, k_near, k_far, sign):
            step = factor * dtv[x]
            for b in range(nv):
                flux = jv[0, 0, b, x] * hb[s, side, 0, near]
                for a in range(1, nv):
                    flux += jv[0, a, b, x] * hb[s, side, a, near]
                total = kk[k_near, x] * hb[s, side, b, near] + kk[k_far, x] * hb[s, side, b, far]
                uh[s, b, x] -= step * (total + sign * flux)

        def rim(x, side, near, k_far):
            step = factor * dtv[x]
            for b in range(nv):
                uh[s, b, x] -= step * (kk[k_far, x] * hb[s, side, b, near])

        @pl.when(has_lo)
        def _():
            halo_up(s).wait_recv()
            edge(0, 0, 1, 0, 1, 0, 0.5)
            rim(1, 0, 1, 0)

        @pl.when(has_hi)
        def _():
            halo_down(s).wait_recv()
            edge(lay - 1, 1, 0, 1, 2, 3, -0.5)
            rim(lay - 2, 1, 0, 3)

        if sending:
            @pl.loop(0, lay)
            def _(x):
                @pl.when(jnp.logical_or(x < first, x >= last))
                def _():
                    send_layer(s, x)

    def home_step(s):
        factor = FACTORS[s - 1]
        ready = 2 * (1 - both) + lay * both

        @pl.loop(0, lay)
        def _(i):
            x = back * i + (1 - back) * (lay - 1 - i)
            wait_bytes(mh.at[s - 1, :, x], mrs.at[s - 1, x])
            step = factor * dtv[x]
            for b in range(nv):
                vp[s, b, 2 + x, mid, :] = uh[s - 1, b, x] - step * mh[s - 1, b, x]

            @pl.when(i == ready - 1)
            def _():
                start_pair(halo_up(s), halo_down(s))

    def mix(s, value):
        @pl.loop(0, nv)
        def _(b):
            weights = [kv[i] for i in range(n)]
            turned = []
            for j in range(groups):
                v = value(b, slice(j * TILE, (j + 1) * TILE))
                turned.append([v] + [pltpu.roll(v, TILE - r * rows, 0) for r in range(1, pack)])
            for k in range(groups):
                total = None
                for j in range(groups):
                    for r in range(pack):
                        term = weights[(j - k) % groups * pack + r] * turned[j][r]
                        total = term if total is None else total + term
                mt[s, b, k * TILE : (k + 1) * TILE, :] = total

        send_home(s)

    def owner_start():
        wait_bytes(tb.at[0, 0:nv], trs.at[0])
        mix(0, lambda b, r: tb[0, b, r, :])

    def owner_step(s):
        wait_bytes(tb.at[s, 0:nv], trs.at[s])
        if s == 1:
            wait_bytes(tb.at[1, nv], trs.at[SECTIONS])
        factor = FACTORS[s - 1]
        mix(s, lambda b, r: tb[s, b, r, :] - factor * (tb[1, nv, r, :] * mt[s - 1, b, r, :]))

    def send_all(s):
        @pl.loop(0, lay)
        def _(x):
            send_layer(s, x)

    local[0].wait()
    local[2].wait()
    local[3].wait()
    pl.semaphore_wait(barrier, n - 1 + lo + hi)

    for p, (x, y) in zip(others, spots):
        send_out(0, p, x, y)
    keep_out(0)
    start_pair(coef_up, coef_down)
    start_pair(halo_up(0), halo_down(0))
    local[1].wait()
    send_steps()
    slope, curve = coupling_tables(n)
    part = lax.broadcasted_iota(jnp.int32, (TILE, nz), 0) // rows
    local[10].wait()
    local[11].wait()
    for j in range(groups):
        for r in range(pack):
            rise = jnp.zeros((TILE, nz), jnp.float32)
            bend = jnp.zeros((TILE, nz), jnp.float32)
            for h in range(pack):
                m = (j * pack + (h + r) % pack - h) % n
                rise = jnp.where(part == h, slope[m], rise)
                bend = jnp.where(part == h, curve[m], bend)
            kv[j * pack + r] = freq[0] * rise + damp[0] * bend
    for s in range(SECTIONS):
        vp[s, :, 2 : 2 + lay, 0:PAD, :] = jnp.zeros((nv, lay, PAD, nz), jnp.float32)
        vp[s, :, 2 : 2 + lay, PAD + ny :, :] = jnp.zeros((nv, lay, PAD, nz), jnp.float32)
        vp[s, :, 0:2, mid, :] = jnp.zeros((nv, 2, ny, nz), jnp.float32)
        vp[s, :, 2 + lay :, mid, :] = jnp.zeros((nv, 2, ny, nz), jnp.float32)
    cy[:, :, 0:PAD, :] = jnp.zeros((2, lay, PAD, nz), jnp.float32)
    cy[:, :, PAD + ny :, :] = jnp.zeros((2, lay, PAD, nz), jnp.float32)

    @pl.when(jnp.logical_not(has_lo))
    def _():
        cx[:, 0:2] = jnp.zeros((2, 2, ny, nz), jnp.float32)

    @pl.when(jnp.logical_not(has_hi))
    def _():
        cx[:, 2 + lay :] = jnp.zeros((2, 2, ny, nz), jnp.float32)

    for c in local[4:10]:
        c.wait()
    stencil_plane()
    land_pair(coef_up, coef_down)
    stencil_layers()
    spatial(0, False)
    owner_start()
    send_all(0)
    home_step(1)
    spatial(1, True)
    owner_step(1)
    owner_step(2)
    home_step(2)
    spatial(2, True)
    home_step(3)
    spatial(3, True)
    owner_step(3)
    owner_step(4)
    home_step(4)
    spatial(4, False)

    @pl.loop(0, lay)
    def _(x):
        wait_bytes(mh.at[4, :, x], mrs.at[4, x])
        step = FACTORS[4] * dtv[x]
        for b in range(nv):
            out[b, x] = uh[4, b, x] - step * mh[4, b, x]

    for unit in range(SECTIONS):
        wait_bytes(tb.at[unit, 0:nv, 0 : (n - 1) * rows, :], ss.at[unit])
        wait_bytes(mt.at[unit, :, 0 : (n - 1) * rows, :], ss.at[SECTIONS + unit])
    wait_bytes(tb.at[1, nv, 0 : (n - 1) * rows, :], ss.at[2 * SECTIONS])
    for s in range(SECTIONS):
        sent_pair(halo_up(s), halo_down(s))
    sent_pair(coef_up, coef_down)


def on_device(n, cells, adjoint, grad, jac, c2, c4, dt, freq, damp):
    nv, lay, ny, nz = adjoint.shape[1:]
    rows = lay * ny // n
    assert rows * n == lay * ny and ny % rows == 0 and lay >= 2
    assert TILE % rows == 0 and (n * rows) % TILE == 0
    f32 = jnp.float32
    anywhere = pl.BlockSpec(memory_space=pl.ANY)
    dma = pltpu.SemaphoreType.DMA
    tall = ny + 2 * PAD
    result = pl.pallas_call(
        functools.partial(kernel, n, cells),
        out_shape=pltpu.VMEM(adjoint.shape[1:], f32),
        in_specs=[anywhere] * 8,
        out_specs=pl.BlockSpec(memory_space=pltpu.VMEM),
        scratch_shapes=[
            pltpu.VMEM((SECTIONS, nv, lay + 4, tall, nz), f32),
            pltpu.VMEM(jac.shape[1:], f32),
            pltpu.VMEM((2, lay + 4, ny, nz), f32),
            pltpu.VMEM((2, lay, tall, nz), f32),
            pltpu.VMEM((2, lay, ny, nz), f32),
            pltpu.VMEM((13, lay, ny, nz), f32),
            pltpu.VMEM((nv, lay, ny, nz), f32),
            pltpu.VMEM((SECTIONS, nv + 1, lay, ny, nz), f32),
            pltpu.VMEM((SECTIONS, nv, lay, ny, nz), f32),
            pltpu.VMEM((SECTIONS, nv + 1, n * rows, nz), f32),
            pltpu.VMEM((SECTIONS, nv, n * rows, nz), f32),
            pltpu.VMEM((SECTIONS, 2, nv, 2, ny, nz), f32),
            pltpu.VMEM((n, TILE, nz), f32),
            pltpu.SMEM((1,), f32),
            pltpu.SMEM((1,), f32),
            dma((12,)),
            dma((2 * SECTIONS + 1,)),
            dma((SECTIONS + 1,)),
            dma((SECTIONS, lay)),
            dma((SECTIONS, 2)),
            dma((SECTIONS, 2)),
            dma((2,)),
            dma((2,)),
        ],
        compiler_params=pltpu.CompilerParams(collective_id=0, has_side_effects=True),
    )(adjoint[0], grad[0], jac[0], c2[0], c4[0], dt[0], freq, damp)
    return result[None]


def solution(mesh):
    placed = (
        P("inst", None, "cells", None, None),
        P("inst", None, "cells", None, None),
        P("inst", None, None, None, "cells", None, None),
        P("inst", None, "cells", None, None),
        P("inst", None, "cells", None, None),
        P("inst", "cells", None, None),
        P(),
        P(),
    )
    return jax.shard_map(
        functools.partial(on_device, mesh.shape["inst"], mesh.shape["cells"]),
        mesh=mesh,
        in_specs=placed,
        out_specs=P("inst", None, "cells", None, None),
        check_vma=False,
    )
```
